128 devices in a mesh: grp: 4 (over z_hi, core), seq: 32 (over y, x, z_lo).
Axes of the slice: x: 4, y: 4, z: 4 (z_hi: 2, z_lo: 2; z = z_hi * 2 + z_lo), core: 2. Of those that a mesh axis runs over, the one named last changes fastest.
Arguments:
- tower_input: bfloat16 [262144, 1024], P(('grp', 'seq')), parts along dimension 0, may hold values from -6 to 6
- first_conv_taps: bfloat16 [3, 1024, 512], replicated, may hold values from -0.109375 to 0.109375
- first_conv_bias: float32 [512], replicated, may hold values from -4 to 4
- first_point_weight: bfloat16 [512, 1024], replicated, may hold values from -0.25 to 0.25
- first_point_bias: float32 [1024], replicated, may hold values from -3 to 3
- second_conv_taps: bfloat16 [3, 1024, 512], replicated, may hold values from -0.109375 to 0.109375
- second_conv_bias: float32 [512], replicated, may hold values from -4 to 4
- second_point_weight: bfloat16 [512, 1024], replicated, may hold values from -0.25 to 0.25
- second_point_bias: float32 [1024], replicated, may hold values from -3 to 3
Outputs:
- tower_out: bfloat16 [262144, 1024], P(('grp', 'seq')), parts along dimension 0
The draws below stay inside these ranges and needn't reach their ends.
There are 4 independent parts, one for each index of `grp`. The reference program is written for one: setup_inputs(seed, part) draws one part's arguments, and reference() takes and returns one part's arrays. A program takes and returns all parts, laid end to end along the dimension named above; an argument that names none is the same for every part. Nothing has to cross between parts.
All inputs are finite; a program needn't handle non-finite values.
Results may differ from the reference program's by a relative error of at most 0.01.
Values may be sent and summed in bfloat16 or wider, within the bound.
No kernel may reach another device: no remote copies, remote signals or barrier semaphores. Data moves between devices by JAX's collectives and lax.ppermute only.
A program may use at most 128 MiB of HBM per device.

```python
import jax
import jax.numpy as jnp
from jax import lax

C = 1024
M = 512
FIRST_DILATION = 512
SECOND_DILATION = 4096
POSITIONS = 65536


def block_levels(key, shape, shards, least, largest):
    def one(axis_at, shards_of):
        steps = jax.random.uniform(jax.random.fold_in(jax.random.fold_in(key, 6), axis_at), (shards_of,), jnp.float32, least / len(shards), largest / len(shards))
        return jnp.repeat(jnp.exp(steps), shape[axis_at] // shards_of).reshape((-1,) + (1,) * (len(shape) - axis_at - 1))

    loudness = one(*shards[0])
    for cut in shards[1:]:
        loudness = loudness * one(*cut)
    return loudness


def gaussian(key, shape, scale, bound, shards=(), held_as=jnp.bfloat16):
    drawn = jax.random.normal(key, shape, jnp.float32) * scale
    if len(shards) > 0:
        drawn = block_levels(key, shape, shards, -0.22, 0.18) * drawn
    return jnp.clip(drawn, min=-bound, max=bound).astype(held_as)


def setup_inputs(seed: int = 0, part: int = 0) -> dict:
    arg_keys = jax.random.split(jax.random.key(seed), 10)
    own_keys = jax.random.split(jax.random.fold_in(arg_keys[9], part), 10)
    tower_input = gaussian(own_keys[0], (POSITIONS, C), 1.0, 6.0, ((0, 32),))
    first_conv_taps = gaussian(arg_keys[1], (3, C, M), (3 * C) ** -0.5, 0.109375)
    first_conv_bias = gaussian(arg_keys[2], (M,), 1.0, 4.0, (), jnp.float32)
    first_point_weight = gaussian(arg_keys[3], (M, C), M ** -0.5, 0.25)
    first_point_bias = gaussian(arg_keys[4], (C,), 0.5, 3.0, (), jnp.float32)
    second_conv_taps = gaussian(arg_keys[5], (3, C, M), (3 * C) ** -0.5, 0.109375)
    second_conv_bias = gaussian(arg_keys[6], (M,), 1.0, 4.0, (), jnp.float32)
    second_point_weight = gaussian(arg_keys[7], (M, C), M ** -0.5, 0.25)
    second_point_bias = gaussian(arg_keys[8], (C,), 0.5, 3.0, (), jnp.float32)
    return {"tower_input": tower_input, "first_conv_taps": first_conv_taps, "first_conv_bias": first_conv_bias, "first_point_weight": first_point_weight, "first_point_bias": first_point_bias, "second_conv_taps": second_conv_taps, "second_conv_bias": second_conv_bias, "second_point_weight": second_point_weight, "second_point_bias": second_point_bias}


def outer_term(acts, tap):
    product = jnp.dot(acts, tap, preferred_element_type=jnp.float32).astype(jnp.bfloat16)
    return lax.optimization_barrier(product).astype(jnp.float32)


def dilated_residual_layer(inputs, taps, bias_conv, point, bias_point, spacing, round_outer):
    acts = jax.nn.gelu(inputs.astype(jnp.float32)).astype(jnp.bfloat16)
    if round_outer:
        total = jnp.roll(outer_term(acts, taps[0]), spacing, axis=0)
        total = total + jnp.dot(acts, taps[1], preferred_element_type=jnp.float32)
        total = total + jnp.roll(outer_term(acts, taps[2]), -spacing, axis=0)
    else:
        total = jnp.dot(jnp.roll(acts, spacing, axis=0), taps[0], preferred_element_type=jnp.float32)
        total = total + jnp.dot(acts, taps[1], preferred_element_type=jnp.float32)
        total = total + jnp.dot(jnp.roll(acts, -spacing, axis=0), taps[2], preferred_element_type=jnp.float32)
    middle = jax.nn.gelu(total + bias_conv).astype(jnp.bfloat16)
    branch = jnp.dot(middle, point, preferred_element_type=jnp.float32)
    return (inputs.astype(jnp.float32) + branch + bias_point).astype(jnp.bfloat16)


def reference(tower_input, first_conv_taps, first_conv_bias, first_point_weight, first_point_bias, second_conv_taps, second_conv_bias, second_point_weight, second_point_bias):
    single_residual_layer = dilated_residual_layer(tower_input, first_conv_taps, first_conv_bias, first_point_weight, first_point_bias, FIRST_DILATION, False)
    return dilated_residual_layer(single_residual_layer, second_conv_taps, second_conv_bias, second_point_weight, second_point_bias, SECOND_DILATION, True)
```

```python
import math

import jax
import jax.numpy as jnp
from jax import lax
from jax.experimental import pallas as pl
from jax.experimental.pallas import tpu as pltpu
from jax.sharding import PartitionSpec as P

BLOCK = 256
LIMIT = 40 * 1024 * 1024
VMEM = pl.BlockSpec(memory_space=pltpu.VMEM)
BF16 = jnp.bfloat16
F32 = jnp.float32


def shift(value, axis, by):
    size = lax.axis_size(axis)
    return lax.ppermute(value, axis, [(i, (i + by) % size) for i in range(size)])


def gelu(v):
    inner = math.sqrt(2.0 / math.pi) * (v + 0.044715 * (v * v * v))
    return 0.5 * v * (1.0 + jnp.tanh(inner))


def dot(a, b):
    return jnp.dot(a, b, preferred_element_type=F32)


def rows_of(step):
    return pl.ds(pl.multiple_of(step * BLOCK, BLOCK), BLOCK)


def params(**kw):
    return pltpu.CompilerParams(vmem_limit_bytes=LIMIT, **kw)


def cost(flops, bytes_accessed):
    return pl.CostEstimate(flops=flops, bytes_accessed=bytes_accessed, transcendentals=0)


def rim_kernel(x_ref, tap_ref, act_ref, first_ref, last_ref):
    act = gelu(x_ref[...].astype(F32)).astype(BF16)
    act_ref[...] = act
    product = dot(act, tap_ref[0]).astype(BF16)

    @pl.when(pl.program_id(0) == 0)
    def _():
        first_ref[...] = product

    @pl.when(pl.program_id(0) == 1)
    def _():
        last_ref[...] = product


def rim(x, taps, spacing):
    rows, c = x.shape
    m = taps.shape[2]
    per = spacing // BLOCK
    jump = (rows - spacing) // BLOCK
    return pl.pallas_call(
        rim_kernel,
        grid=(2, per),
        in_specs=[
            pl.BlockSpec((BLOCK, c), lambda e, h: (jump * e + h, 0)),
            pl.BlockSpec((1, c, m), lambda e, h: (2 - 2 * e, 0, 0)),
        ],
        out_specs=[
            pl.BlockSpec((BLOCK, c), lambda e, h: (per * e + h, 0)),
            pl.BlockSpec((BLOCK, m), lambda e, h: (h + e * (per - 1 - h), 0)),
            pl.BlockSpec((BLOCK, m), lambda e, h: (e * h, 0)),
        ],
        out_shape=[
            jax.ShapeDtypeStruct((2 * spacing, c), BF16),
            jax.ShapeDtypeStruct((spacing, m), BF16),
            jax.ShapeDtypeStruct((spacing, m), BF16),
        ],
        compiler_params=params(),
        cost_estimate=cost(4 * spacing * c * m, 8 * spacing * c),
        name="rim",
    )(x, taps)


def after_total(total, x, bias_conv, point, bias_point, outer, refs, at):
    one_ref, act_ref, out0_ref, out2_ref = refs
    mid = gelu(total + bias_conv[...]).astype(BF16)
    one = (x.astype(F32) + dot(mid, point[...]) + bias_point[...]).astype(BF16)
    one_ref[at, :] = one
    act = gelu(one.astype(F32)).astype(BF16)
    act_ref[at, :] = act
    out0_ref[at, :] = dot(act, outer[0]).astype(BF16)
    out2_ref[at, :] = dot(act, outer[2]).astype(BF16)


def inner_kernel(
    per, x_ref, edge_ref, taps, bias_conv, point, bias_point, outer,
    near_ref, one_ref, act_ref, out0_ref, out2_ref,
):
    @pl.loop(0, 2 * per)
    def _(s):
        near_ref[rows_of(s), :] = gelu(x_ref[rows_of(s + per), :].astype(F32)).astype(BF16)

    refs = (one_ref, act_ref, out0_ref, out2_ref)

    @pl.loop(0, per)
    def _(s):
        total = dot(edge_ref[rows_of(s), :], taps[0])
        total = total + dot(near_ref[rows_of(s), :], taps[1])
        total = total + dot(near_ref[rows_of(s + per), :], taps[2])
        after_total(
            total, x_ref[rows_of(s + per), :], bias_conv, point, bias_point, outer, refs, rows_of(s)
        )

    @pl.loop(0, per)
    def _(s):
        total = dot(near_ref[rows_of(s), :], taps[0])
        total = total + dot(near_ref[rows_of(s + per), :], taps[1])
        total = total + dot(edge_ref[rows_of(s + per), :], taps[2])
        after_total(
            total, x_ref[rows_of(s + 2 * per), :], bias_conv, point, bias_point, outer, refs,
            rows_of(s + per),
        )


def edge_kernel(
    per, x_ref, edge_ref, near_ref, prev_ref, next_ref, taps, bias_conv, point, bias_point, outer,
    one_ref, act_ref, out0_ref, out2_ref,
):
    refs = (one_ref, act_ref, out0_ref, out2_ref)

    @pl.loop(0, per)
    def _(s):
        total = prev_ref[rows_of(s), :].astype(F32)
        total = total + dot(edge_ref[rows_of(s), :], taps[1])
        total = total + dot(near_ref[rows_of(s), :], taps[2])
        after_total(
            total, x_ref[rows_of(s), :], bias_conv, point, bias_point, outer, refs, rows_of(s)
        )

    @pl.loop(0, per)
    def _(s):
        total = dot(near_ref[rows_of(s + per), :], taps[0])
        total = total + dot(edge_ref[rows_of(s + per), :], taps[1])
        total = total + next_ref[rows_of(s), :].astype(F32)
        after_total(
            total, x_ref[rows_of(s + 3 * per), :], bias_conv, point, bias_point, outer, refs,
            rows_of(s + per),
        )


def layer_outputs(rows, c, m):
    return [
        jax.ShapeDtypeStruct((rows, c), BF16),
        jax.ShapeDtypeStruct((rows, c), BF16),
        jax.ShapeDtypeStruct((rows, m), BF16),
        jax.ShapeDtypeStruct((rows, m), BF16),
    ]


def inner(x, edge, taps, bias_conv, point, bias_point, outer, spacing):
    c, m = taps.shape[1:]
    rows = 2 * spacing

    def body(*refs):
        inner_kernel(spacing // BLOCK, *refs)

    return pl.pallas_call(
        body,
        in_specs=[VMEM] * 7,
        out_specs=[VMEM] * 5,
        out_shape=[jax.ShapeDtypeStruct((rows, c), BF16)] + layer_outputs(rows, c, m),
        compiler_params=params(),
        cost_estimate=cost(12 * rows * c * m, 10 * rows * c),
        name="inner",
    )(x, edge, taps, bias_conv, point, bias_point, outer)


def edges(x, edge, near, prev, following, taps, bias_conv, point, bias_point, outer, spacing):
    c, m = taps.shape[1:]
    rows = 2 * spacing

    def body(*refs):
        edge_kernel(spacing // BLOCK, *refs)

    return pl.pallas_call(
        body,
        in_specs=[VMEM] * 10,
        out_specs=[VMEM] * 4,
        out_shape=layer_outputs(rows, c, m),
        compiler_params=params(),
        cost_estimate=cost(10 * rows * c * m, 10 * rows * c),
        name="edges",
    )(x, edge, near, prev, following, taps, bias_conv, point, bias_point, outer)


def centre_kernel(act_ref, tap, bias_conv, out_ref):
    @pl.loop(0, act_ref.shape[0] // BLOCK)
    def _(s):
        out_ref[rows_of(s), :] = dot(act_ref[rows_of(s), :], tap[1]) + bias_conv[...]


def centre(act, outer, bias_conv):
    rows, c = act.shape
    m = outer.shape[2]
    return pl.pallas_call(
        centre_kernel,
        in_specs=[VMEM] * 3,
        out_specs=VMEM,
        out_shape=jax.ShapeDtypeStruct((rows, m), F32),
        compiler_params=params(),
        cost_estimate=cost(2 * rows * c * m, 4 * rows * c),
        name="centre",
    )(act, outer, bias_conv)


def finish_kernel(centre_ref, back_ref, ahead_ref, one_ref, point, bias_point, *rest):
    out_ref = rest[-1]
    at = rows_of(pl.program_id(0))
    total = centre_ref[at, :] + back_ref[at, :].astype(F32) + ahead_ref[at, :].astype(F32)
    mid = gelu(total).astype(BF16)
    out = one_ref[at, :].astype(F32) + dot(mid, point[...]) + bias_point[...]
    out_ref[...] = out.astype(BF16)


def finish(mid_sum, back, ahead, one, point, bias_point, whole, rows, block_of):
    c = one.shape[1]
    m = back.shape[1]
    own = one.shape[0]
    extra = [] if whole is None else [whole]
    return pl.pallas_call(
        finish_kernel,
        grid=(own // BLOCK,),
        in_specs=[VMEM] * 6 + [pl.BlockSpec(memory_space=pl.ANY)] * len(extra),
        out_specs=pl.BlockSpec((BLOCK, c), lambda s: (block_of(s), 0)),
        out_shape=jax.ShapeDtypeStruct((rows, c), BF16),
        input_output_aliases={6: 0} if extra else {},
        compiler_params=params(),
        cost_estimate=cost(2 * own * c * m, 8 * own * c),
        name="finish",
    )(mid_sum, back, ahead, one, point, bias_point, *extra)


def per_device(
    tower_input,
    first_conv_taps,
    first_conv_bias,
    first_point_weight,
    first_point_bias,
    second_conv_taps,
    second_conv_bias,
    second_point_weight,
    second_point_bias,
):
    rows = tower_input.shape[0]
    spacing = rows // 4
    per = spacing // BLOCK
    conv1, point1 = first_conv_bias[None, :], first_point_bias[None, :]
    conv2, point2 = second_conv_bias[None, :], second_point_bias[None, :]

    edge_act, first, last = rim(tower_input, first_conv_taps, spacing)
    following = shift(first, "seq", -1)
    prev = shift(last, "seq", 1)
    near, one_a, act_a, a0, a2 = inner(
        tower_input, edge_act, first_conv_taps, conv1, first_point_weight, point1, second_conv_taps, spacing
    )
    back_a = shift(a0, "seq", 2)
    ahead_a = shift(a2, "seq", -2)
    one_b, act_b, b0, b2 = edges(
        tower_input, edge_act, near, prev, following, first_conv_taps, conv1, first_point_weight, point1,
        second_conv_taps, spacing,
    )
    back_b = shift(b0, "seq", 2)
    ahead_b = shift(b2, "seq", -2)
    centre_a = centre(act_a, second_conv_taps, conv2)
    centre_b = centre(act_b, second_conv_taps, conv2)
    out = finish(
        centre_a, back_a, ahead_a, one_a, second_point_weight, point2, None, rows, lambda s: s + per
    )
    return finish(
        centre_b, back_b, ahead_b, one_b, second_point_weight, point2, out, rows,
        lambda s: s + 2 * per * (s // per),
    )


def solution(mesh):
    return jax.shard_map(
        per_device,
        mesh=mesh,
        in_specs=(P(("grp", "seq"), None), P(), P(), P(), P(), P(), P(), P(), P()),
        out_specs=P(("grp", "seq"), None),
        check_vma=False,
    )
```

```python
import math

import jax
import jax.numpy as jnp
from jax import lax
from jax.experimental import pallas as pl
from jax.experimental.pallas import tpu as pltpu
from jax.sharding import PartitionSpec as P

LIMIT = 16 * 1024 * 1024
VMEM = pl.BlockSpec(memory_space=pltpu.VMEM)
ANY = pl.BlockSpec(memory_space=pl.ANY)
HBM = pl.BlockSpec(memory_space=pltpu.HBM)
BF16 = jnp.bfloat16
F32 = jnp.float32


def swap(value, first, step):
    size = lax.axis_size("seq")
    pairs = []
    for i in range(size):
        if first(i):
            j = (i + step) % size
            pairs += [(i, j), (j, i)]
    return lax.ppermute(value, "seq", sorted(pairs))


def gelu(v):
    inner = math.sqrt(2.0 / math.pi) * (v + 0.044715 * (v * v * v))
    return 0.5 * v * (1.0 + jnp.tanh(inner))


def dot(a, b):
    return jnp.dot(a, b, preferred_element_type=F32)


def odd_position():
    return lax.rem(lax.axis_index("seq"), 2)


def quarter_rows(quarter, size):
    at = quarter + odd_position() * (3 - 2 * quarter)
    return pl.ds(pl.multiple_of(at * size, size), size)


def call(body, name, out_shape, args, flops, scratch, aliases=None, out_specs=None, specs=None):
    moved = sum(a.size * a.dtype.itemsize for a in args)
    return pl.pallas_call(
        body,
        in_specs=specs,
        out_specs=[VMEM] * len(out_shape) if out_specs is None else out_specs,
        out_shape=out_shape,
        scratch_shapes=scratch,
        input_output_aliases=aliases or {},
        compiler_params=pltpu.CompilerParams(vmem_limit_bytes=LIMIT),
        cost_estimate=pl.CostEstimate(flops=flops, bytes_accessed=moved, transcendentals=0),
        name=name,
    )(*args)


def shape(rows, columns, dtype=BF16):
    return jax.ShapeDtypeStruct((rows, columns), dtype)


def rim(x, taps, quarter):
    size, (c, m) = x.shape[0] // 4, taps.shape[1:]
    tap = 2 if quarter == 0 else 0

    def body(x_hbm, taps_hbm, act_ref, product_ref, x_own, tap_own, sems):
        which = tap + odd_position() * (2 - 2 * tap)
        half = size // 2
        rows = quarter_rows(quarter, size)
        copies = [
            pltpu.make_async_copy(x_hbm.at[rows], x_own, sems.at[0]),
            pltpu.make_async_copy(taps_hbm.at[which], tap_own, sems.at[1]),
        ]
        for copy in copies:
            copy.start()
        copies[0].wait()
        for k in range(2):
            part = pl.ds(k * half, half)
            act_ref[part, :] = gelu(x_own[part, :].astype(F32)).astype(BF16)
        copies[1].wait()
        product_ref[...] = dot(act_ref[...], tap_own[...]).astype(BF16)

    return call(
        body, f"rim{quarter}", [shape(size, c), shape(size, m)], (x, taps), 2 * size * c * m,
        [pltpu.VMEM((size, c), BF16), pltpu.VMEM((c, m), BF16), pltpu.SemaphoreType.DMA((2,))],
        specs=[HBM, HBM],
    )


def after_total(total, x, point, bias_point, outer, one_ref, act_ref, first_ref, second_ref):
    mid = gelu(total).astype(BF16)
    one = (x.astype(F32) + dot(mid, point[...]) + bias_point[...]).astype(BF16)
    one_ref[...] = one
    act = gelu(one.astype(F32)).astype(BF16)
    act_ref[...] = act
    odd_pair = lax.rem(lax.div(lax.axis_index("seq"), 2), 2)
    first_ref[...] = dot(act, outer[2 * odd_pair]).astype(BF16)
    second_ref[...] = dot(act, outer[2 - 2 * odd_pair]).astype(BF16)


def layer(x, quarter, acts, arrived, weights, fresh=False):
    taps, bias_conv, point, bias_point, outer = weights
    size, (c, m) = x.shape[0] // 4, taps.shape[1:]
    given = [a for a in acts if a is not None]
    known = [a is not None for a in acts]
    loads = (quarter, quarter + 1) if fresh else (quarter,)

    def body(*refs):
        refs = list(refs)
        x_hbm = refs.pop(0)
        sources = [refs.pop(0) if k else None for k in known]
        arrived_ref = None if arrived is None else refs.pop(0)
        taps_ref, bias_conv_ref, point_ref, bias_point_ref, outer_ref = refs[:5]
        refs = refs[5:]
        made = [refs.pop(0), refs.pop(0)] if fresh else []
        one_ref, act_ref, first_ref, second_ref = refs[:4]
        x_own, sems = refs[4:]
        copies = [
            pltpu.make_async_copy(x_hbm.at[quarter_rows(q, size)], x_own.at[k], sems.at[k])
            for k, q in enumerate(loads)
        ]
        for copy in copies:
            copy.start()
        if fresh:
            for k in range(2):
                copies[k].wait()
                made[k][...] = gelu(x_own[k].astype(F32)).astype(BF16)
            sources[1:] = made
        odd = odd_position()
        total = None if arrived is None else arrived_ref[...].astype(F32)
        for k, source in enumerate(sources):
            if source is not None:
                term = dot(source[...], taps_ref[k + odd * (2 - 2 * k)])
                total = term if total is None else total + term
        if not fresh:
            copies[0].wait()
        after_total(
            total + bias_conv_ref[...], x_own[0], point_ref, bias_point_ref, outer_ref, one_ref, act_ref, first_ref,
            second_ref,
        )

    args = [x] + given + ([] if arrived is None else [arrived]) + list(weights)
    outs = ([shape(size, c)] * 2 if fresh else []) + [shape(size, c)] * 2 + [shape(size, m)] * 2
    return call(
        body, f"layer{quarter}", outs, args, 12 * size * c * m,
        [pltpu.VMEM((len(loads), size, c), BF16), pltpu.SemaphoreType.DMA((len(loads),))],
        specs=[HBM] + [VMEM] * (len(args) - 1),
    )


def centre(acts, outer, bias_conv):
    size, c = acts[0].shape
    m = outer.shape[2]
    n = len(acts)

    def body(*refs):
        outer_ref, bias_ref = refs[n : n + 2]
        for act_ref, out_ref in zip(refs[:n], refs[n + 2 :]):
            out_ref[...] = dot(act_ref[...], outer_ref[1]) + bias_ref[...]

    args = list(acts) + [outer, bias_conv]
    return call(body, "centre", [shape(size, m, F32)] * n, args, 2 * n * size * c * m, [], specs=[VMEM] * len(args))


def finish(quarter, centre_sum, one_side, other_side, one, point, bias_point, whole):
    size, c = one.shape
    m = centre_sum.shape[1]
    half = size // 2

    def body(centre_ref, one_side_ref, other_side_ref, one_ref, point_ref, bias_ref, *rest):
        out_hbm, held, sems = rest[-3:]
        start = quarter_rows(quarter, size).start
        copies = []
        for k in range(2):
            part = pl.ds(k * half, half)
            total = centre_ref[part, :] + one_side_ref[part, :].astype(F32) + other_side_ref[part, :].astype(F32)
            mid = gelu(total).astype(BF16)
            out = one_ref[part, :].astype(F32) + dot(mid, point_ref[...]) + bias_ref[...]
            held[k] = out.astype(BF16)
            to = pl.ds(pl.multiple_of(start + k * half, half), half)
            copies.append(pltpu.make_async_copy(held.at[k], out_hbm.at[to], sems.at[k]))
            copies[k].start()
        for copy in copies:
            copy.wait()

    args = [centre_sum, one_side, other_side, one, point, bias_point] + ([] if whole is None else [whole])
    return call(
        body, f"finish{quarter}", [shape(4 * size, c)], args, 2 * size * c * m,
        [pltpu.VMEM((2, half, c), BF16), pltpu.SemaphoreType.DMA((2,))],
        aliases={} if whole is None else {6: 0}, out_specs=[ANY], specs=[VMEM] * 6 + [ANY] * (len(args) - 6),
    )[0]


def per_device(
    tower_input,
    first_conv_taps,
    first_conv_bias,
    first_point_weight,
    first_point_bias,
    second_conv_taps,
    second_conv_bias,
    second_point_weight,
    second_point_bias,
):
    near = (first_conv_taps, first_conv_bias[None, :], first_point_weight, first_point_bias[None, :], second_conv_taps)

    tower_input = pltpu.with_memory_space_constraint(tower_input, pltpu.HBM)
    rim_taps = pltpu.with_memory_space_constraint(first_conv_taps, pltpu.HBM)
    act0, to_pair = rim(tower_input, rim_taps, 0)
    later, to_pair = lax.optimization_barrier((tower_input, to_pair))
    from_pair = swap(to_pair, lambda i: i % 2 == 1, 1)
    act3, to_partner = rim(later, rim_taps, 3)
    from_partner = swap(to_partner, lambda i: i % 2 == 0, 1)

    def send(products):
        return (
            swap(products[0], lambda i: i // 2 % 2 == 0, 2),
            swap(products[1], lambda i: i // 2 % 2 == 1, 2),
        )

    act1, act2, one1, far1, *products1 = layer(tower_input, 1, (act0, None, None), None, near, fresh=True)
    sides1 = send(products1)
    one2, far2, *products2 = layer(tower_input, 2, (act1, act2, act3), None, near)
    sides2 = send(products2)
    one3, far3, *products3 = layer(tower_input, 3, (act2, act3, None), from_partner, near)
    sides3 = send(products3)
    one0, far0, *products0 = layer(tower_input, 0, (None, act0, act1), from_pair, near)
    sides0 = send(products0)

    centres = centre((far1, far2, far3, far0), second_conv_taps, second_conv_bias[None, :])
    out = None
    for quarter, total, sides, one in zip((1, 2, 3, 0), centres, (sides1, sides2, sides3, sides0), (one1, one2, one3, one0)):
        out = finish(quarter, total, *sides, one, second_point_weight, second_point_bias[None, :], out)
    return out


def solution(mesh):
    return jax.shard_map(
        per_device,
        mesh=mesh,
        in_specs=(P(("grp", "seq"), None), P(), P(), P(), P(), P(), P(), P(), P()),
        out_specs=P(("grp", "seq"), None),
        check_vma=False,
    )
```

```python
import math

import jax
import jax.numpy as jnp
from jax import lax
from jax.experimental import pallas as pl
from jax.experimental.pallas import tpu as pltpu
from jax.sharding import PartitionSpec as P

LIMIT = 16 * 1024 * 1024
VMEM = pl.BlockSpec(memory_space=pltpu.VMEM)
ANY = pl.BlockSpec(memory_space=pl.ANY)
HBM = pl.BlockSpec(memory_space=pltpu.HBM)
BF16 = jnp.bfloat16
F32 = jnp.float32


def swap(value, first, step):
    size = lax.axis_size("seq")
    pairs = []
    for i in range(size):
        if first(i):
            j = (i + step) % size
            pairs += [(i, j), (j, i)]
    return lax.ppermute(value, "seq", sorted(pairs))


def gelu(v):
    inner = math.sqrt(2.0 / math.pi) * (v + 0.044715 * (v * v * v))
    return 0.5 * v * (1.0 + jnp.tanh(inner))


def dot(a, b):
    return jnp.dot(a, b, preferred_element_type=F32)


def odd_position():
    return lax.rem(lax.axis_index("seq"), 2)


def quarter_rows(quarter, size):
    at = quarter + odd_position() * (3 - 2 * quarter)
    return pl.ds(pl.multiple_of(at * size, size), size)


def call(body, name, out_shape, args, flops, scratch, aliases=None, out_specs=None, specs=None):
    moved = sum(a.size * a.dtype.itemsize for a in args)
    return pl.pallas_call(
        body,
        in_specs=specs,
        out_specs=[VMEM] * len(out_shape) if out_specs is None else out_specs,
        out_shape=out_shape,
        scratch_shapes=scratch,
        input_output_aliases=aliases or {},
        compiler_params=pltpu.CompilerParams(vmem_limit_bytes=LIMIT),
        cost_estimate=pl.CostEstimate(flops=flops, bytes_accessed=moved, transcendentals=0),
        name=name,
    )(*args)


def shape(rows, columns, dtype=BF16):
    return jax.ShapeDtypeStruct((rows, columns), dtype)


def rim(x, taps, quarter):
    size, (c, m) = x.shape[0] // 4, taps.shape[1:]
    tap = 2 if quarter == 0 else 0

    def body(x_hbm, taps_hbm, act_ref, product_ref, x_own, tap_own, sems):
        which = tap + odd_position() * (2 - 2 * tap)
        piece = size // 4
        start = quarter_rows(quarter, size).start
        copies = []
        for k in range(4):
            rows = pl.ds(pl.multiple_of(start + k * piece, piece), piece)
            copies.append(pltpu.make_async_copy(x_hbm.at[rows], x_own.at[pl.ds(k * piece, piece)], sems.at[k]))
        copies.insert(2, pltpu.make_async_copy(taps_hbm.at[which], tap_own, sems.at[4]))
        for copy in copies:
            copy.start()
        tap_copy = copies.pop(2)
        for k in range(4):
            copies[k].wait()
            part = pl.ds(k * piece, piece)
            act_ref[part, :] = gelu(x_own[part, :].astype(F32)).astype(BF16)
        tap_copy.wait()
        product_ref[...] = dot(act_ref[...], tap_own[...]).astype(BF16)

    return call(
        body, f"rim{quarter}", [shape(size, c), shape(size, m)], (x, taps), 2 * size * c * m,
        [pltpu.VMEM((size, c), BF16), pltpu.VMEM((c, m), BF16), pltpu.SemaphoreType.DMA((5,))],
        specs=[HBM, HBM],
    )


def after_total(total, x, point, bias_point, outer, one_ref, act_ref, first_ref, second_ref):
    mid = gelu(total).astype(BF16)
    one = (x.astype(F32) + dot(mid, point[...]) + bias_point[...]).astype(BF16)
    one_ref[...] = one
    act = gelu(one.astype(F32)).astype(BF16)
    act_ref[...] = act
    odd_pair = lax.rem(lax.div(lax.axis_index("seq"), 2), 2)
    first_ref[...] = dot(act, outer[2 * odd_pair]).astype(BF16)
    second_ref[...] = dot(act, outer[2 - 2 * odd_pair]).astype(BF16)


def layer(x, quarter, acts, arrived, weights, fresh=False):
    taps, bias_conv, point, bias_point, outer = weights
    size, (c, m) = x.shape[0] // 4, taps.shape[1:]
    given = [a for a in acts if a is not None]
    known = [a is not None for a in acts]
    loads = (quarter, quarter + 1) if fresh else (quarter,)

    def body(*refs):
        refs = list(refs)
        x_hbm = refs.pop(0)
        sources = [refs.pop(0) if k else None for k in known]
        arrived_ref = None if arrived is None else refs.pop(0)
        taps_ref, bias_conv_ref, point_ref, bias_point_ref, outer_ref = refs[:5]
        refs = refs[5:]
        made = [refs.pop(0), refs.pop(0)] if fresh else []
        one_ref, act_ref, first_ref, second_ref = refs[:4]
        x_own, sems = refs[4:]
        copies = [
            pltpu.make_async_copy(x_hbm.at[quarter_rows(q, size)], x_own.at[k], sems.at[k])
            for k, q in enumerate(loads)
        ]
        for copy in copies:
            copy.start()
        if fresh:
            for k in range(2):
                copies[k].wait()
                made[k][...] = gelu(x_own[k].astype(F32)).astype(BF16)
            sources[1:] = made
        odd = odd_position()
        total = None if arrived is None else arrived_ref[...].astype(F32)
        for k, source in enumerate(sources):
            if source is not None:
                term = dot(source[...], taps_ref[k + odd * (2 - 2 * k)])
                total = term if total is None else total + term
        if not fresh:
            copies[0].wait()
        after_total(
            total + bias_conv_ref[...], x_own[0], point_ref, bias_point_ref, outer_ref, one_ref, act_ref, first_ref,
            second_ref,
        )

    args = [x] + given + ([] if arrived is None else [arrived]) + list(weights)
    outs = ([shape(size, c)] * 2 if fresh else []) + [shape(size, c)] * 2 + [shape(size, m)] * 2
    return call(
        body, f"layer{quarter}", outs, args, 12 * size * c * m,
        [pltpu.VMEM((len(loads), size, c), BF16), pltpu.SemaphoreType.DMA((len(loads),))],
        specs=[HBM] + [VMEM] * (len(args) - 1),
    )


def centre(acts, outer, bias_conv):
    size, c = acts[0].shape
    m = outer.shape[2]
    n = len(acts)

    def body(*refs):
        outer_ref, bias_ref = refs[n : n + 2]
        for act_ref, out_ref in zip(refs[:n], refs[n + 2 :]):
            out_ref[...] = dot(act_ref[...], outer_ref[1]) + bias_ref[...]

    args = list(acts) + [outer, bias_conv]
    return call(body, "centre", [shape(size, m, F32)] * n, args, 2 * n * size * c * m, [], specs=[VMEM] * len(args))


def finish(quarter, centre_sum, one_side, other_side, one, point, bias_point, whole):
    size, c = one.shape
    m = centre_sum.shape[1]
    half = size // 2

    def body(centre_ref, one_side_ref, other_side_ref, one_ref, point_ref, bias_ref, *rest):
        out_hbm, held, sems = rest[-3:]
        start = quarter_rows(quarter, size).start
        copies = []
        for k in range(2):
            part = pl.ds(k * half, half)
            total = centre_ref[part, :] + one_side_ref[part, :].astype(F32) + other_side_ref[part, :].astype(F32)
            mid = gelu(total).astype(BF16)
            out = one_ref[part, :].astype(F32) + dot(mid, point_ref[...]) + bias_ref[...]
            held[k] = out.astype(BF16)
            to = pl.ds(pl.multiple_of(start + k * half, half), half)
            copies.append(pltpu.make_async_copy(held.at[k], out_hbm.at[to], sems.at[k]))
            copies[k].start()
        for copy in copies:
            copy.wait()

    args = [centre_sum, one_side, other_side, one, point, bias_point] + ([] if whole is None else [whole])
    return call(
        body, f"finish{quarter}", [shape(4 * size, c)], args, 2 * size * c * m,
        [pltpu.VMEM((2, half, c), BF16), pltpu.SemaphoreType.DMA((2,))],
        aliases={} if whole is None else {6: 0}, out_specs=[ANY], specs=[VMEM] * 6 + [ANY] * (len(args) - 6),
    )[0]


def per_device(
    tower_input,
    first_conv_taps,
    first_conv_bias,
    first_point_weight,
    first_point_bias,
    second_conv_taps,
    second_conv_bias,
    second_point_weight,
    second_point_bias,
):
    near = (first_conv_taps, first_conv_bias[None, :], first_point_weight, first_point_bias[None, :], second_conv_taps)

    tower_input = pltpu.with_memory_space_constraint(tower_input, pltpu.HBM)
    rim_taps = pltpu.with_memory_space_constraint(first_conv_taps, pltpu.HBM)
    act0, to_pair = rim(tower_input, rim_taps, 0)
    from_pair = swap(to_pair, lambda i: i % 2 == 1, 1)

    def send(products):
        return (
            swap(products[1], lambda i: i // 2 % 2 == 1, 2),
            swap(products[0], lambda i: i // 2 % 2 == 0, 2),
        )

    act1, act2, one1, far1, *products1 = layer(tower_input, 1, (act0, None, None), None, near, fresh=True)
    later, *products1 = lax.optimization_barrier((tower_input, *products1))
    sides1 = send(products1)
    act3, to_partner = rim(later, rim_taps, 3)
    from_partner = swap(to_partner, lambda i: i % 2 == 0, 1)
    one2, far2, *products2 = layer(tower_input, 2, (act1, act2, act3), None, near)
    sides2 = send(products2)
    one0, far0, *products0 = layer(tower_input, 0, (None, act0, act1), from_pair, near)
    sides0 = send(products0)
    one3, far3, *products3 = layer(tower_input, 3, (act2, act3, None), from_partner, near)
    sides3 = send(products3)

    centres = centre((far1, far2, far0, far3), second_conv_taps, second_conv_bias[None, :])
    out = None
    for quarter, total, sides, one in zip(
        (1, 2, 0, 3), centres, (sides1, sides2, sides0, sides3), (one1, one2, one0, one3)
    ):
        out = finish(quarter, total, *sides, one, second_point_weight, second_point_bias[None, :], out)
    return out


def solution(mesh):
    return jax.shard_map(
        per_device,
        mesh=mesh,
        in_specs=(P(("grp", "seq"), None), P(), P(), P(), P(), P(), P(), P(), P()),
        out_specs=P(("grp", "seq"), None),
        check_vma=False,
    )
```

```python
import math

import jax
import jax.numpy as jnp
from jax import lax
from jax.experimental import pallas as pl
from jax.experimental.pallas import tpu as pltpu
from jax.sharding import PartitionSpec as P

LIMIT = 16 * 1024 * 1024
VMEM = pl.BlockSpec(memory_space=pltpu.VMEM)
ANY = pl.BlockSpec(memory_space=pl.ANY)
HBM = pl.BlockSpec(memory_space=pltpu.HBM)
SLOPE = math.sqrt(2.0 / math.pi)
LAST_PIECE = 128
BF16 = jnp.bfloat16
F32 = jnp.float32


def swap(value, first, step):
    size = lax.axis_size("seq")
    pairs = []
    for i in range(size):
        if first(i):
            j = (i + step) % size
            pairs += [(i, j), (j, i)]
    return lax.ppermute(value, "seq", sorted(pairs))


def gelu(v):
    half = 0.5 * v
    return half + half * jnp.tanh(v * (SLOPE + (SLOPE * 0.044715) * (v * v)))


def dot(a, b):
    return jnp.dot(a, b, preferred_element_type=F32)


def odd_position():
    return lax.rem(lax.axis_index("seq"), 2)


def quarter_rows(quarter, size):
    at = quarter + odd_position() * (3 - 2 * quarter)
    return pl.ds(pl.multiple_of(at * size, size), size)


def call(body, name, out_shape, args, flops, scratch, aliases=None, out_specs=None, specs=None):
    moved = sum(a.size * a.dtype.itemsize for a in args)
    return pl.pallas_call(
        body,
        in_specs=specs,
        out_specs=[VMEM] * len(out_shape) if out_specs is None else out_specs,
        out_shape=out_shape,
        scratch_shapes=scratch,
        input_output_aliases=aliases or {},
        compiler_params=pltpu.CompilerParams(vmem_limit_bytes=LIMIT),
        cost_estimate=pl.CostEstimate(flops=flops, bytes_accessed=moved, transcendentals=0),
        name=name,
    )(*args)


def shape(rows, columns, dtype=BF16):
    return jax.ShapeDtypeStruct((rows, columns), dtype)


def rim(x, taps, quarter):
    size, (c, m) = x.shape[0] // 4, taps.shape[1:]
    half = size // 2
    top, bottom = pl.ds(0, half), pl.ds(half, half)
    tap = 2 if quarter == 0 else 0

    def body(x_ref, taps_ref, act_ref, product_ref, x_own, tap_own, sems):
        which = tap + odd_position() * (2 - 2 * tap)
        start = quarter_rows(quarter, size).start

        def rows(k):
            return pl.ds(pl.multiple_of(start + k * half, half), half)

        first, tap_copy, second = (
            pltpu.make_async_copy(x_ref.at[rows(0)], x_own.at[top], sems.at[0]),
            pltpu.make_async_copy(taps_ref.at[which], tap_own, sems.at[1]),
            pltpu.make_async_copy(x_ref.at[rows(1)], x_own.at[bottom], sems.at[2]),
        )
        for copy in (first, tap_copy, second):
            copy.start()
        first.wait()
        act_ref[top, :] = gelu(x_own[top, :].astype(F32)).astype(BF16)
        tap_copy.wait()
        second.wait()
        product_ref[top, :] = dot(act_ref[top, :], tap_own[...]).astype(BF16)
        act_ref[bottom, :] = gelu(x_own[bottom, :].astype(F32)).astype(BF16)
        product_ref[bottom, :] = dot(act_ref[bottom, :], tap_own[...]).astype(BF16)

    return call(
        body, f"rim{quarter}", [shape(size, c), shape(size, m)], (x, taps), 2 * size * c * m,
        [pltpu.VMEM((size, c), BF16), pltpu.VMEM((c, m), BF16), pltpu.SemaphoreType.DMA((3,))],
        specs=[HBM] * 2,
    )


def after_total(total, x, point, bias_point, outer, one_ref, act_ref, product_refs):
    mid = gelu(total).astype(BF16)
    one = (x.astype(F32) + dot(mid, point[...]) + bias_point[...]).astype(BF16)
    one_ref[...] = one
    act = gelu(one.astype(F32)).astype(BF16)
    act_ref[...] = act
    odd_pair = lax.rem(lax.div(lax.axis_index("seq"), 2), 2)
    for tap, pieces in zip((2 * odd_pair, 2 - 2 * odd_pair), product_refs):
        product = dot(act, outer[tap]).astype(BF16)
        at = 0
        for ref in pieces:
            ref[...] = product[at : at + ref.shape[0], :]
            at += ref.shape[0]


def layer(x, quarter, acts, arrived, weights, pieces, fresh=False):
    taps, bias_conv, point, bias_point, outer = weights
    size, (c, m) = x.shape[0] // 4, taps.shape[1:]
    given = [a for a in acts if a is not None]
    known = [a is not None for a in acts]
    loads = (quarter, quarter + 1) if fresh else (quarter,)
    n = len(pieces)

    def body(*refs):
        refs = list(refs)
        x_ref = refs.pop(0)
        sources = [refs.pop(0) if k else None for k in known]
        arrived_ref = None if arrived is None else refs.pop(0)
        taps_ref, bias_conv_ref, point_ref, bias_point_ref, outer_ref = refs[:5]
        refs = refs[5:]
        made = [refs.pop(0), refs.pop(0)] if fresh else []
        one_ref, act_ref = refs[:2]
        product_refs = refs[2 : 2 + n], refs[2 + n : 2 + 2 * n]
        x_own, sems = refs[2 + 2 * n :]
        odd = odd_position()
        copies = [
            pltpu.make_async_copy(x_ref.at[quarter_rows(q, size)], x_own.at[k], sems.at[k]) for k, q in enumerate(loads)
        ]
        for copy in copies:
            copy.start()
        total = None if arrived is None else arrived_ref[...].astype(F32)
        for k, source in enumerate(sources):
            if fresh and k > 0:
                source = made[k - 1]
                copies[k - 1].wait()
                source[...] = gelu(x_own[k - 1].astype(F32)).astype(BF16)
            if source is not None:
                term = dot(source[...], taps_ref[k + odd * (2 - 2 * k)])
                total = term if total is None else total + term
        if not fresh:
            copies[0].wait()
        after_total(
            total + bias_conv_ref[...], x_own[0], point_ref, bias_point_ref, outer_ref, one_ref, act_ref, product_refs
        )

    args = [x] + given + ([] if arrived is None else [arrived]) + list(weights)
    outs = ([shape(size, c)] * 2 if fresh else []) + [shape(size, c)] * 2 + [shape(rows, m) for rows in pieces] * 2
    results = call(
        body, f"layer{quarter}", outs, args, 12 * size * c * m,
        [pltpu.VMEM((len(loads), size, c), BF16), pltpu.SemaphoreType.DMA((len(loads),))],
        specs=[HBM] + [VMEM] * (len(args) - 1),
    )
    return *results[: -2 * n], list(zip(results[-2 * n : -n], results[-n:]))


def centre(acts, outer, bias_conv):
    size, c = acts[0].shape
    m = outer.shape[2]
    n = len(acts)

    def body(*refs):
        outer_ref, bias_ref = refs[n : n + 2]
        for act_ref, out_ref in zip(refs[:n], refs[n + 2 :]):
            out_ref[...] = dot(act_ref[...], outer_ref[1]) + bias_ref[...]

    args = list(acts) + [outer, bias_conv]
    return call(body, "centre", [shape(size, m, F32)] * n, args, 2 * n * size * c * m, [], specs=[VMEM] * len(args))


def finish(quarter, at, centre_sum, one_side, other_side, one, point, bias_point, whole):
    size, c = one.shape
    rows, m = one_side.shape
    steps = 2 if rows % 256 == 0 else 1
    step = rows // steps

    def body(centre_ref, one_side_ref, other_side_ref, one_ref, point_ref, bias_ref, *rest):
        out_hbm, held, sems = rest[-3:]
        start = quarter_rows(quarter, size).start + at
        copies = []
        for k in range(steps):
            part, own = pl.ds(k * step, step), pl.ds(at + k * step, step)
            total = centre_ref[own, :] + one_side_ref[part, :].astype(F32) + other_side_ref[part, :].astype(F32)
            mid = gelu(total).astype(BF16)
            out = one_ref[own, :].astype(F32) + dot(mid, point_ref[...]) + bias_ref[...]
            held[k] = out.astype(BF16)
            to = pl.ds(pl.multiple_of(start + k * step, 128), step)
            copies.append(pltpu.make_async_copy(held.at[k], out_hbm.at[to], sems.at[k]))
            copies[k].start()
        for copy in copies:
            copy.wait()

    args = [centre_sum, one_side, other_side, one, point, bias_point] + ([] if whole is None else [whole])
    return call(
        body, f"finish{quarter}", [shape(4 * size, c)], args, 2 * rows * c * m,
        [pltpu.VMEM((steps, step, c), BF16), pltpu.SemaphoreType.DMA((steps,))],
        aliases={} if whole is None else {6: 0}, out_specs=[ANY], specs=[VMEM] * 6 + [ANY] * (len(args) - 6),
    )[0]


def per_device(
    tower_input,
    first_conv_taps,
    first_conv_bias,
    first_point_weight,
    first_point_bias,
    second_conv_taps,
    second_conv_bias,
    second_point_weight,
    second_point_bias,
):
    size = tower_input.shape[0] // 4
    whole = (size,)
    split = (size - LAST_PIECE, LAST_PIECE)

    near = (first_conv_taps, first_conv_bias[None, :], first_point_weight, first_point_bias[None, :], second_conv_taps)
    x = pltpu.with_memory_space_constraint(tower_input, pltpu.HBM)
    rim_taps = pltpu.with_memory_space_constraint(first_conv_taps, pltpu.HBM)
    act0, to_pair = rim(x, rim_taps, 0)
    from_pair = swap(to_pair, lambda i: i % 2 == 1, 1)

    def send(products):
        return [
            (swap(second, lambda i: i // 2 % 2 == 1, 2), swap(first, lambda i: i // 2 % 2 == 0, 2))
            for first, second in products
        ]

    act1, act2, one1, far1, products1 = layer(x, 1, (act0, None, None), None, near, whole, fresh=True)
    later, products1 = lax.optimization_barrier((x, products1))
    sides1 = send(products1)
    act3, to_partner = rim(later, rim_taps, 3)
    from_partner = swap(to_partner, lambda i: i % 2 == 0, 1)
    one2, far2, products2 = layer(x, 2, (act1, act2, act3), None, near, whole)
    sides2 = send(products2)
    one0, far0, products0 = layer(x, 0, (None, act0, act1), from_pair, near, whole)
    sides0 = send(products0)
    one3, far3, products3 = layer(x, 3, (act2, act3, None), from_partner, near, split)
    sides3 = send(products3)

    centres = centre((far1, far2, far0, far3), second_conv_taps, second_conv_bias[None, :])
    out = None
    for quarter, total, sides, one in zip(
        (1, 2, 0, 3), centres, (sides1, sides2, sides0, sides3), (one1, one2, one0, one3)
    ):
        at = 0
        for pair in sides:
            out = finish(quarter, at, total, *pair, one, second_point_weight, second_point_bias[None, :], out)
            at += pair[0].shape[0]
    return out


def solution(mesh):
    return jax.shard_map(
        per_device,
        mesh=mesh,
        in_specs=(P(("grp", "seq"), None), P(), P(), P(), P(), P(), P(), P(), P()),
        out_specs=P(("grp", "seq"), None),
        check_vma=False,
    )
```

```python
import math

import jax
import jax.numpy as jnp
from jax import lax
from jax.experimental import pallas as pl
from jax.experimental.pallas import tpu as pltpu
from jax.sharding import PartitionSpec as P

LIMIT = 16 * 1024 * 1024
VMEM = pl.BlockSpec(memory_space=pltpu.VMEM)
ANY = pl.BlockSpec(memory_space=pl.ANY)
HBM = pl.BlockSpec(memory_space=pltpu.HBM)
SLOPE = math.sqrt(2.0 / math.pi)
LAST_PIECE = 256
BF16 = jnp.bfloat16
F32 = jnp.float32


def swap(value, first, step):
    size = lax.axis_size("seq")
    pairs = []
    for i in range(size):
        if first(i):
            j = (i + step) % size
            pairs += [(i, j), (j, i)]
    return lax.ppermute(value, "seq", sorted(pairs))


def gelu(v):
    half = 0.5 * v
    return half + half * jnp.tanh(v * (SLOPE + (SLOPE * 0.044715) * (v * v)))


def dot(a, b):
    return jnp.dot(a, b, preferred_element_type=F32)


def odd_position():
    return lax.rem(lax.axis_index("seq"), 2)


def quarter_rows(quarter, size):
    at = quarter + odd_position() * (3 - 2 * quarter)
    return pl.ds(pl.multiple_of(at * size, size), size)


def call(body, name, out_shape, args, flops, scratch, aliases=None, out_specs=None, specs=None):
    moved = sum(a.size * a.dtype.itemsize for a in args)
    return pl.pallas_call(
        body,
        in_specs=specs,
        out_specs=[VMEM] * len(out_shape) if out_specs is None else out_specs,
        out_shape=out_shape,
        scratch_shapes=scratch,
        input_output_aliases=aliases or {},
        compiler_params=pltpu.CompilerParams(vmem_limit_bytes=LIMIT),
        cost_estimate=pl.CostEstimate(flops=flops, bytes_accessed=moved, transcendentals=0),
        name=name,
    )(*args)


def shape(rows, columns, dtype=BF16):
    return jax.ShapeDtypeStruct((rows, columns), dtype)


def rim(x, taps, quarter):
    size, (c, m) = x.shape[0] // 4, taps.shape[1:]
    half = size // 2
    top, bottom = pl.ds(0, half), pl.ds(half, half)
    tap = 2 if quarter == 0 else 0

    def body(x_ref, taps_ref, act_ref, product_ref, x_own, tap_own, sems):
        which = tap + odd_position() * (2 - 2 * tap)
        start = quarter_rows(quarter, size).start

        def rows(k):
            return pl.ds(pl.multiple_of(start + k * half, half), half)

        first, tap_copy, second = (
            pltpu.make_async_copy(x_ref.at[rows(0)], x_own.at[top], sems.at[0]),
            pltpu.make_async_copy(taps_ref.at[which], tap_own, sems.at[1]),
            pltpu.make_async_copy(x_ref.at[rows(1)], x_own.at[bottom], sems.at[2]),
        )
        for copy in (first, tap_copy, second):
            copy.start()
        first.wait()
        act_ref[top, :] = gelu(x_own[top, :].astype(F32)).astype(BF16)
        tap_copy.wait()
        second.wait()
        product_ref[top, :] = dot(act_ref[top, :], tap_own[...]).astype(BF16)
        act_ref[bottom, :] = gelu(x_own[bottom, :].astype(F32)).astype(BF16)
        product_ref[bottom, :] = dot(act_ref[bottom, :], tap_own[...]).astype(BF16)

    return call(
        body, f"rim{quarter}", [shape(size, c), shape(size, m)], (x, taps), 2 * size * c * m,
        [pltpu.VMEM((size, c), BF16), pltpu.VMEM((c, m), BF16), pltpu.SemaphoreType.DMA((3,))],
        specs=[HBM] * 2,
    )


def after_total(total, x, point, bias_point, outer, one_ref, act_ref, product_refs):
    mid = gelu(total).astype(BF16)
    one = (x.astype(F32) + dot(mid, point[...]) + bias_point[...]).astype(BF16)
    one_ref[...] = one
    act = gelu(one.astype(F32)).astype(BF16)
    act_ref[...] = act
    odd_pair = lax.rem(lax.div(lax.axis_index("seq"), 2), 2)
    for tap, pieces in zip((2 * odd_pair, 2 - 2 * odd_pair), product_refs):
        product = dot(act, outer[tap]).astype(BF16)
        at = 0
        for ref in pieces:
            ref[...] = product[at : at + ref.shape[0], :]
            at += ref.shape[0]


def layer(x, quarter, acts, arrived, weights, pieces, fresh=False):
    taps, bias_conv, point, bias_point, outer = weights
    size, (c, m) = x.shape[0] // 4, taps.shape[1:]
    given = [a for a in acts if a is not None]
    known = [a is not None for a in acts]
    loads = (quarter, quarter + 1) if fresh else (quarter,)
    n = len(pieces)

    def body(*refs):
        refs = list(refs)
        x_ref = refs.pop(0)
        sources = [refs.pop(0) if k else None for k in known]
        arrived_ref = None if arrived is None else refs.pop(0)
        taps_ref, bias_conv_ref, point_ref, bias_point_ref, outer_ref = refs[:5]
        refs = refs[5:]
        made = [refs.pop(0), refs.pop(0)] if fresh else []
        one_ref, act_ref = refs[:2]
        product_refs = refs[2 : 2 + n], refs[2 + n : 2 + 2 * n]
        x_own, sems = refs[2 + 2 * n :]
        odd = odd_position()
        copies = [
            pltpu.make_async_copy(x_ref.at[quarter_rows(q, size)], x_own.at[k], sems.at[k]) for k, q in enumerate(loads)
        ]
        for copy in copies:
            copy.start()
        total = None if arrived is None else arrived_ref[...].astype(F32)
        for k, source in enumerate(sources):
            if fresh and k > 0:
                source = made[k - 1]
                copies[k - 1].wait()
                source[...] = gelu(x_own[k - 1].astype(F32)).astype(BF16)
            if source is not None:
                term = dot(source[...], taps_ref[k + odd * (2 - 2 * k)])
                total = term if total is None else total + term
        if not fresh:
            copies[0].wait()
        after_total(
            total + bias_conv_ref[...], x_own[0], point_ref, bias_point_ref, outer_ref, one_ref, act_ref, product_refs
        )

    args = [x] + given + ([] if arrived is None else [arrived]) + list(weights)
    outs = ([shape(size, c)] * 2 if fresh else []) + [shape(size, c)] * 2 + [shape(rows, m) for rows in pieces] * 2
    results = call(
        body, f"layer{quarter}", outs, args, 12 * size * c * m,
        [pltpu.VMEM((len(loads), size, c), BF16), pltpu.SemaphoreType.DMA((len(loads),))],
        specs=[HBM] + [VMEM] * (len(args) - 1),
    )
    return *results[: -2 * n], list(zip(results[-2 * n : -n], results[-n:]))


def centre(acts, outer, bias_conv):
    size, c = acts[0].shape
    m = outer.shape[2]
    n = len(acts)

    def body(*refs):
        outer_ref, bias_ref = refs[n : n + 2]
        for act_ref, out_ref in zip(refs[:n], refs[n + 2 :]):
            out_ref[...] = dot(act_ref[...], outer_ref[1]) + bias_ref[...]

    args = list(acts) + [outer, bias_conv]
    return call(body, "centre", [shape(size, m, F32)] * n, args, 2 * n * size * c * m, [], specs=[VMEM] * len(args))


def finish(quarter, at, centre_sum, one_side, other_side, one, point, bias_point, whole):
    size, c = one.shape
    rows, m = one_side.shape
    steps = 2 if rows % 32 == 0 else 1
    step = rows // steps

    def body(centre_ref, one_side_ref, other_side_ref, one_ref, point_ref, bias_ref, *rest):
        out_hbm, held, sems = rest[-3:]
        start = quarter_rows(quarter, size).start + at
        copies = []
        for k in range(steps):
            part, own = pl.ds(k * step, step), pl.ds(at + k * step, step)
            total = centre_ref[own, :] + one_side_ref[part, :].astype(F32) + other_side_ref[part, :].astype(F32)
            mid = gelu(total).astype(BF16)
            out = one_ref[own, :].astype(F32) + dot(mid, point_ref[...]) + bias_ref[...]
            held[k] = out.astype(BF16)
            to = pl.ds(pl.multiple_of(start + k * step, 16), step)
            copies.append(pltpu.make_async_copy(held.at[k], out_hbm.at[to], sems.at[k]))
            copies[k].start()
        for copy in copies:
            copy.wait()

    args = [centre_sum, one_side, other_side, one, point, bias_point] + ([] if whole is None else [whole])
    return call(
        body, f"finish{quarter}", [shape(4 * size, c)], args, 2 * rows * c * m,
        [pltpu.VMEM((steps, step, c), BF16), pltpu.SemaphoreType.DMA((steps,))],
        aliases={} if whole is None else {6: 0}, out_specs=[ANY], specs=[VMEM] * 6 + [ANY] * (len(args) - 6),
    )[0]


def per_device(
    tower_input,
    first_conv_taps,
    first_conv_bias,
    first_point_weight,
    first_point_bias,
    second_conv_taps,
    second_conv_bias,
    second_point_weight,
    second_point_bias,
):
    size = tower_input.shape[0] // 4
    whole = (size,)
    split = (size - LAST_PIECE, LAST_PIECE)

    near = (first_conv_taps, first_conv_bias[None, :], first_point_weight, first_point_bias[None, :], second_conv_taps)
    x = pltpu.with_memory_space_constraint(tower_input, pltpu.HBM)
    rim_taps = pltpu.with_memory_space_constraint(first_conv_taps, pltpu.HBM)
    act0, to_pair = rim(x, rim_taps, 0)
    from_pair = swap(to_pair, lambda i: i % 2 == 1, 1)

    def send(products):
        return [
            (swap(second, lambda i: i // 2 % 2 == 1, 2), swap(first, lambda i: i // 2 % 2 == 0, 2))
            for first, second in products
        ]

    act1, act2, one1, far1, products1 = layer(x, 1, (act0, None, None), None, near, whole, fresh=True)
    later, products1 = lax.optimization_barrier((x, products1))
    sides1 = send(products1)
    act3, to_partner = rim(later, rim_taps, 3)
    from_partner = swap(to_partner, lambda i: i % 2 == 0, 1)
    one2, far2, products2 = layer(x, 2, (act1, act2, act3), None, near, whole)
    sides2 = send(products2)
    one0, far0, products0 = layer(x, 0, (None, act0, act1), from_pair, near, whole)
    sides0 = send(products0)
    one3, far3, products3 = layer(x, 3, (act2, act3, None), from_partner, near, split)
    sides3 = send(products3[:1])

    def finished(quarter, at, total, sides, one, out):
        for pair in sides:
            out = finish(quarter, at, total, *pair, one, second_point_weight, second_point_bias[None, :], out)
            at += pair[0].shape[0]
        return out

    total1, total2, total0, total3 = centre((far1, far2, far0, far3), second_conv_taps, second_conv_bias[None, :])
    out = finished(1, 0, total1, sides1, one1, None)
    out = finished(2, 0, total2, sides2, one2, out)
    out, last = lax.optimization_barrier((out, products3[1]))
    sides3 += send([last])
    out = finished(0, 0, total0, sides0, one0, out)
    return finished(3, 0, total3, sides3, one3, out)


def solution(mesh):
    return jax.shard_map(
        per_device,
        mesh=mesh,
        in_specs=(P(("grp", "seq"), None), P(), P(), P(), P(), P(), P(), P(), P()),
        out_specs=P(("grp", "seq"), None),
        check_vma=False,
    )
```

```python
import math

import jax
import jax.numpy as jnp
from jax import lax
from jax.experimental import pallas as pl
from jax.experimental.pallas import tpu as pltpu
from jax.sharding import PartitionSpec as P

LIMIT = 16 * 1024 * 1024
VMEM = pl.BlockSpec(memory_space=pltpu.VMEM)
ANY = pl.BlockSpec(memory_space=pl.ANY)
HBM = pl.BlockSpec(memory_space=pltpu.HBM)
SLOPE = math.sqrt(2.0 / math.pi)
LAST_PIECE = 128
RELAY = 128
BF16 = jnp.bfloat16
F32 = jnp.float32


def swap(value, first, step):
    size = lax.axis_size("seq")
    pairs = []
    for i in range(size):
        if first(i):
            j = (i + step) % size
            pairs += [(i, j), (j, i)]
    return lax.ppermute(value, "seq", sorted(pairs))


def gelu(v):
    half = 0.5 * v
    return half + half * jnp.tanh(v * (SLOPE + (SLOPE * 0.044715) * (v * v)))


def dot(a, b):
    return jnp.dot(a, b, preferred_element_type=F32)


def odd_position():
    return lax.rem(lax.axis_index("seq"), 2)


def quarter_rows(quarter, size):
    at = quarter + odd_position() * (3 - 2 * quarter)
    return pl.ds(pl.multiple_of(at * size, size), size)


def call(body, name, out_shape, args, flops, scratch, aliases=None, out_specs=None, specs=None):
    moved = sum(a.size * a.dtype.itemsize for a in args)
    return pl.pallas_call(
        body,
        in_specs=specs,
        out_specs=[VMEM] * len(out_shape) if out_specs is None else out_specs,
        out_shape=out_shape,
        scratch_shapes=scratch,
        input_output_aliases=aliases or {},
        compiler_params=pltpu.CompilerParams(vmem_limit_bytes=LIMIT),
        cost_estimate=pl.CostEstimate(flops=flops, bytes_accessed=moved, transcendentals=0),
        name=name,
    )(*args)


def shape(rows, columns, dtype=BF16):
    return jax.ShapeDtypeStruct((rows, columns), dtype)


def rim_activations(x_ref, taps_ref, tap, quarter, act_ref, x_own, tap_own, sems, put):
    size = x_own.shape[0]
    half = size // 2
    top, bottom = pl.ds(0, half), pl.ds(half, half)
    which = tap + odd_position() * (2 - 2 * tap)
    start = quarter_rows(quarter, size).start
    copies = []
    for k in range(2):
        rows = pl.ds(pl.multiple_of(start + k * half, half), half)
        copies.append(pltpu.make_async_copy(x_ref.at[rows], x_own.at[pl.ds(k * half, half)], sems.at[k]))
    copies.insert(1, pltpu.make_async_copy(taps_ref.at[which], tap_own, sems.at[2]))
    for copy in copies:
        copy.start()
    copies[0].wait()
    act_ref[top, :] = gelu(x_own[top, :].astype(F32)).astype(BF16)
    copies[1].wait()
    copies[2].wait()
    put(0, dot(act_ref[top, :], tap_own[...]).astype(BF16))
    act_ref[bottom, :] = gelu(x_own[bottom, :].astype(F32)).astype(BF16)
    put(1, dot(act_ref[bottom, :], tap_own[...]).astype(BF16))


def rim_scratch(size, c, m):
    return [pltpu.VMEM((size, c), BF16), pltpu.VMEM((c, m), BF16), pltpu.SemaphoreType.DMA((3,))]


def pair_rim(x, taps):
    size, (c, m) = x.shape[0] // 4, taps.shape[1:]
    half = size // 2

    def body(x_ref, taps_ref, act_ref, direct_ref, relay_ref, *scratch):
        def put(k, product):
            if k == 0:
                direct_ref[:half, :] = product
            else:
                direct_ref[half:, :] = product[: half - RELAY, :]
                relay_ref[...] = product[half - RELAY :, :]

        rim_activations(x_ref, taps_ref, 2, 0, act_ref, *scratch, put)

    return call(
        body, "rim0", [shape(size, c), shape(size - RELAY, m), shape(RELAY, m)], (x, taps), 2 * size * c * m,
        rim_scratch(size, c, m), specs=[HBM] * 2,
    )


def partner_rim(x, taps):
    size, (c, m) = x.shape[0] // 4, taps.shape[1:]
    half = size // 2

    def body(x_ref, taps_ref, act_ref, product_ref, *scratch):
        def put(k, product):
            product_ref[k * half : (k + 1) * half, :] = product

        rim_activations(x_ref, taps_ref, 0, 3, act_ref, *scratch, put)

    return call(
        body, "rim3", [shape(size, c), shape(size, m)], (x, taps), 2 * size * c * m, rim_scratch(size, c, m),
        specs=[HBM] * 2,
    )


def first_product(far, outer):
    size, c = far.shape
    m = outer.shape[2]

    def body(far_ref, outer_ref, first_ref):
        first_ref[...] = dot(far_ref[...], outer_ref[2 * odd_pair()]).astype(BF16)

    return call(body, "first1", [shape(size, m)], (far, outer), 2 * size * c * m, [], specs=[VMEM] * 2)[0]


def odd_pair():
    return lax.rem(lax.div(lax.axis_index("seq"), 2), 2)


def first_quarter(x, act, weights):
    taps, bias_conv, point, bias_point, outer = weights
    size, (c, m) = x.shape[0] // 4, taps.shape[1:]

    def body(
        x_ref, before_ref, taps_ref, bias_conv_ref, point_hbm, bias_point_ref, outer_hbm,
        act1_ref, act2_ref, one_ref, far_ref, second_ref, point_own, outer_own, sems,
    ):
        copies = [
            pltpu.make_async_copy(point_hbm, point_own, sems.at[0]),
            pltpu.make_async_copy(outer_hbm.at[2 - 2 * odd_pair()], outer_own, sems.at[1]),
        ]
        for copy in copies:
            copy.start()
        odd = odd_position()
        total = dot(before_ref[...], taps_ref[2 * odd])
        act1_ref[...] = gelu(x_ref[quarter_rows(1, size), :].astype(F32)).astype(BF16)
        total = total + dot(act1_ref[...], taps_ref[1])
        act2_ref[...] = gelu(x_ref[quarter_rows(2, size), :].astype(F32)).astype(BF16)
        total = total + dot(act2_ref[...], taps_ref[2 - 2 * odd])
        mid = gelu(total + bias_conv_ref[...]).astype(BF16)
        copies[0].wait()
        one = x_ref[quarter_rows(1, size), :].astype(F32) + dot(mid, point_own[...]) + bias_point_ref[...]
        one = one.astype(BF16)
        one_ref[...] = one
        far = gelu(one.astype(F32)).astype(BF16)
        far_ref[...] = far
        copies[1].wait()
        second_ref[...] = dot(far, outer_own[...]).astype(BF16)

    point, outer = (pltpu.with_memory_space_constraint(w, pltpu.HBM) for w in (point, outer))
    args = (x, act, taps, bias_conv, point, bias_point, outer)
    return call(
        body, "layer1", [shape(size, c)] * 4 + [shape(size, m)], args, 10 * size * c * m,
        [pltpu.VMEM((m, c), BF16), pltpu.VMEM((c, m), BF16), pltpu.SemaphoreType.DMA((2,))],
        specs=[VMEM] * 4 + [HBM, VMEM, HBM],
    )


def after_total(total, x, point, bias_point, outer, one_ref, act_ref, product_refs):
    mid = gelu(total).astype(BF16)
    one = (x.astype(F32) + dot(mid, point[...]) + bias_point[...]).astype(BF16)
    one_ref[...] = one
    act = gelu(one.astype(F32)).astype(BF16)
    act_ref[...] = act
    odd = odd_pair()
    for tap, pieces in zip((2 * odd, 2 - 2 * odd), product_refs):
        product = dot(act, outer[tap]).astype(BF16)
        at = 0
        for ref in pieces:
            ref[...] = product[at : at + ref.shape[0], :]
            at += ref.shape[0]


def layer(x, quarter, acts, arrived, weights, pieces):
    taps, bias_conv, point, bias_point, outer = weights
    size, (c, m) = x.shape[0] // 4, taps.shape[1:]
    given = [a for a in acts if a is not None]
    known = [a is not None for a in acts]
    n = len(pieces)

    def body(*refs):
        refs = list(refs)
        x_ref = refs.pop(0)
        sources = [refs.pop(0) if k else None for k in known]
        arrived_refs = [refs.pop(0) for _ in arrived]
        taps_ref, bias_conv_ref, point_ref, bias_point_ref, outer_ref = refs[:5]
        refs = refs[5:]
        one_ref, act_ref = refs[:2]
        product_refs = refs[2 : 2 + n], refs[2 + n : 2 + 2 * n]
        x_own, sem = refs[2 + 2 * n :]
        odd = odd_position()
        copy = pltpu.make_async_copy(x_ref.at[quarter_rows(quarter, size)], x_own, sem)
        copy.start()
        total = None
        for k, source in enumerate(sources):
            if source is not None:
                term = dot(source[...], taps_ref[k + odd * (2 - 2 * k)])
                total = term if total is None else total + term
        if arrived:
            parts, missing = [], size
            for ref, (_, first) in zip(arrived_refs, arrived):
                rows = min(ref.shape[0] - first, missing)
                parts.append(ref[first : first + rows, :].astype(F32))
                missing -= rows
            total = total + (parts[0] if len(parts) == 1 else jnp.concatenate(parts, axis=0))
        copy.wait()
        after_total(
            total + bias_conv_ref[...], x_own[...], point_ref, bias_point_ref, outer_ref, one_ref, act_ref, product_refs
        )

    args = [x] + given + [value for value, _ in arrived] + list(weights)
    outs = [shape(size, c)] * 2 + [shape(rows, m) for rows in pieces] * 2
    results = call(
        body, f"layer{quarter}", outs, args, 12 * size * c * m,
        [pltpu.VMEM((size, c), BF16), pltpu.SemaphoreType.DMA],
        specs=[HBM] + [VMEM] * (len(args) - 1),
    )
    return *results[: -2 * n], list(zip(results[-2 * n : -n], results[-n:]))


def centre(acts, outer, bias_conv):
    size, c = acts[0].shape
    m = outer.shape[2]
    n = len(acts)

    def body(*refs):
        outer_ref, bias_ref = refs[n : n + 2]
        for act_ref, out_ref in zip(refs[:n], refs[n + 2 :]):
            out_ref[...] = dot(act_ref[...], outer_ref[1]) + bias_ref[...]

    args = list(acts) + [outer, bias_conv]
    return call(body, "centre", [shape(size, m, F32)] * n, args, 2 * n * size * c * m, [], specs=[VMEM] * len(args))


def finish(quarter, at, centre_sum, one_side, other_side, one, point, bias_point, whole):
    size, c = one.shape
    rows, m = one_side.shape
    steps = 2 if rows % 256 == 0 else 1
    step = rows // steps

    def body(centre_ref, one_side_ref, other_side_ref, one_ref, point_ref, bias_ref, *rest):
        out_hbm, held, sems = rest[-3:]
        start = quarter_rows(quarter, size).start + at
        copies = []
        for k in range(steps):
            part, own = pl.ds(k * step, step), pl.ds(at + k * step, step)
            total = centre_ref[own, :] + one_side_ref[part, :].astype(F32) + other_side_ref[part, :].astype(F32)
            mid = gelu(total).astype(BF16)
            out = one_ref[own, :].astype(F32) + dot(mid, point_ref[...]) + bias_ref[...]
            held[k] = out.astype(BF16)
            to = pl.ds(pl.multiple_of(start + k * step, 128), step)
            copies.append(pltpu.make_async_copy(held.at[k], out_hbm.at[to], sems.at[k]))
            copies[k].start()
        for copy in copies:
            copy.wait()

    args = [centre_sum, one_side, other_side, one, point, bias_point] + ([] if whole is None else [whole])
    return call(
        body, f"finish{quarter}", [shape(4 * size, c)], args, 2 * rows * c * m,
        [pltpu.VMEM((steps, step, c), BF16), pltpu.SemaphoreType.DMA((steps,))],
        aliases={} if whole is None else {6: 0}, out_specs=[ANY], specs=[VMEM] * 6 + [ANY] * (len(args) - 6),
    )[0]


def per_device(
    tower_input,
    first_conv_taps,
    first_conv_bias,
    first_point_weight,
    first_point_bias,
    second_conv_taps,
    second_conv_bias,
    second_point_weight,
    second_point_bias,
):
    size = tower_input.shape[0] // 4
    whole = (size,)
    split = (size - LAST_PIECE, LAST_PIECE)

    near = (first_conv_taps, first_conv_bias[None, :], first_point_weight, first_point_bias[None, :], second_conv_taps)
    x = pltpu.with_memory_space_constraint(tower_input, pltpu.HBM)
    rim_taps = pltpu.with_memory_space_constraint(first_conv_taps, pltpu.HBM)

    def to_partner(value):
        return swap(value, lambda i: i % 2 == 0, 1)

    def second_matching(value):
        return swap(value, lambda i: i // 2 % 2 == 1, 2)

    def first_matching(value):
        return swap(value, lambda i: i // 2 % 2 == 0, 2)

    def send(products):
        return [(second_matching(second), first_matching(first)) for first, second in products]

    act0, direct, relay = pair_rim(x, rim_taps)
    handed = to_partner(relay)
    from_pair = swap(direct, lambda i: i % 2 == 1, 1)
    near_input, handed = lax.optimization_barrier((tower_input, handed))
    relayed = swap(handed, lambda i: i % 2 == 0, 3)

    act1, act2, one1, far1, second1 = first_quarter(near_input, act0, near)
    far1, second1 = lax.optimization_barrier((far1, second1))
    side1 = second_matching(second1)
    later, relayed, first1 = lax.optimization_barrier((x, relayed, first_product(far1, second_conv_taps)))
    returned = to_partner(relayed)
    sides1 = [(side1, first_matching(first1))]
    act3, for_partner = partner_rim(later, rim_taps)
    from_partner = to_partner(for_partner)
    one2, far2, products2 = layer(x, 2, (act1, act2, act3), [], near, whole)
    sides2 = send(products2)
    one0, far0, products0 = layer(
        x, 0, (None, act0, act1), [(from_pair, 0), (returned, 0)], near, whole
    )
    sides0 = send(products0)
    one3, far3, products3 = layer(x, 3, (act2, act3, None), [(from_partner, 0)], near, split)
    sides3 = send(products3)

    centres = centre((far1, far2, far0, far3), second_conv_taps, second_conv_bias[None, :])
    out = None
    for quarter, total, sides, one in zip(
        (1, 2, 0, 3), centres, (sides1, sides2, sides0, sides3), (one1, one2, one0, one3)
    ):
        at = 0
        for pair in sides:
            out = finish(quarter, at, total, *pair, one, second_point_weight, second_point_bias[None, :], out)
            at += pair[0].shape[0]
    return out


def solution(mesh):
    return jax.shard_map(
        per_device,
        mesh=mesh,
        in_specs=(P(("grp", "seq"), None), P(), P(), P(), P(), P(), P(), P(), P()),
        out_specs=P(("grp", "seq"), None),
        check_vma=False,
    )
```

```python
import math

import jax
import jax.numpy as jnp
from jax import lax
from jax.experimental import pallas as pl
from jax.experimental.pallas import tpu as pltpu
from jax.sharding import PartitionSpec as P

LIMIT = 16 * 1024 * 1024
VMEM = pl.BlockSpec(memory_space=pltpu.VMEM)
ANY = pl.BlockSpec(memory_space=pl.ANY)
HBM = pl.BlockSpec(memory_space=pltpu.HBM)
SLOPE = math.sqrt(2.0 / math.pi)
LAST_PIECE = 128
LATE = 128
BF16 = jnp.bfloat16
F32 = jnp.float32


def swap(value, first, step):
    size = lax.axis_size("seq")
    pairs = []
    for i in range(size):
        if first(i):
            j = (i + step) % size
            pairs += [(i, j), (j, i)]
    return lax.ppermute(value, "seq", sorted(pairs))


def gelu(v):
    half = 0.5 * v
    return half + half * jnp.tanh(v * (SLOPE + (SLOPE * 0.044715) * (v * v)))


def dot(a, b):
    return jnp.dot(a, b, preferred_element_type=F32)


def odd_position():
    return lax.rem(lax.axis_index("seq"), 2)


def quarter_rows(quarter, size):
    at = quarter + odd_position() * (3 - 2 * quarter)
    return pl.ds(pl.multiple_of(at * size, size), size)


def call(body, name, out_shape, args, flops, scratch, aliases=None, out_specs=None, specs=None):
    moved = sum(a.size * a.dtype.itemsize for a in args)
    return pl.pallas_call(
        body,
        in_specs=specs,
        out_specs=[VMEM] * len(out_shape) if out_specs is None else out_specs,
        out_shape=out_shape,
        scratch_shapes=scratch,
        input_output_aliases=aliases or {},
        compiler_params=pltpu.CompilerParams(vmem_limit_bytes=LIMIT),
        cost_estimate=pl.CostEstimate(flops=flops, bytes_accessed=moved, transcendentals=0),
        name=name,
    )(*args)


def shape(rows, columns, dtype=BF16):
    return jax.ShapeDtypeStruct((rows, columns), dtype)


def rim_activations(x_ref, taps_ref, tap, quarter, size, act_ref, product_ref, x_own, tap_own, sems):
    rows = x_own.shape[0]
    half = size // 2
    top, bottom = pl.ds(0, half), pl.ds(half, rows - half)
    which = tap + odd_position() * (2 - 2 * tap)
    start = quarter_rows(quarter, size).start
    copies = [
        pltpu.make_async_copy(x_ref.at[pl.ds(pl.multiple_of(start, half), half)], x_own.at[top], sems.at[0]),
        pltpu.make_async_copy(taps_ref.at[which], tap_own, sems.at[1]),
        pltpu.make_async_copy(
            x_ref.at[pl.ds(pl.multiple_of(start + half, half), rows - half)], x_own.at[bottom], sems.at[2]
        ),
    ]
    for copy in copies:
        copy.start()
    copies[0].wait()
    act_ref[top, :] = gelu(x_own[top, :].astype(F32)).astype(BF16)
    copies[1].wait()
    copies[2].wait()
    product_ref[top, :] = dot(act_ref[top, :], tap_own[...]).astype(BF16)
    act_ref[bottom, :] = gelu(x_own[bottom, :].astype(F32)).astype(BF16)
    product_ref[bottom, :] = dot(act_ref[bottom, :], tap_own[...]).astype(BF16)


def rim(x, taps, quarter, rows):
    size, (c, m) = x.shape[0] // 4, taps.shape[1:]

    def body(x_ref, taps_ref, act_ref, product_ref, *scratch):
        tap = 2 if quarter == 0 else 0
        rim_activations(x_ref, taps_ref, tap, quarter, size, act_ref, product_ref, *scratch)

    return call(
        body, f"rim{quarter}", [shape(rows, c), shape(rows, m)], (x, taps), 2 * rows * c * m,
        [pltpu.VMEM((rows, c), BF16), pltpu.VMEM((c, m), BF16), pltpu.SemaphoreType.DMA((3,))], specs=[HBM] * 2,
    )


def behind_first(far, outer, act_top, act_bottom, taps):
    size, c = far.shape
    m = outer.shape[2]
    late = act_bottom.shape[0]

    def body(far_ref, outer_ref, top_ref, bottom_ref, taps_ref, first_ref, late_ref, act_ref):
        first_ref[...] = dot(far_ref[...], outer_ref[2 * odd_pair()]).astype(BF16)
        late_ref[...] = dot(bottom_ref[...], taps_ref[2 - 2 * odd_position()]).astype(BF16)
        act_ref[: size - late, :] = top_ref[...]
        act_ref[size - late :, :] = bottom_ref[...]

    return call(
        body, "behind1", [shape(size, m), shape(late, m), shape(size, c)], (far, outer, act_top, act_bottom, taps),
        2 * size * c * m, [], specs=[VMEM] * 5,
    )


def odd_pair():
    return lax.rem(lax.div(lax.axis_index("seq"), 2), 2)


def first_quarter(x, act, weights):
    taps, bias_conv, point, bias_point, outer = weights
    size, (c, m) = x.shape[0] // 4, taps.shape[1:]

    def body(
        x_ref, before_ref, taps_ref, bias_conv_ref, point_hbm, bias_point_ref, outer_hbm,
        bottom_ref, act1_ref, act2_ref, one_ref, far_ref, second_ref, point_own, outer_own, sems,
    ):
        copies = [
            pltpu.make_async_copy(point_hbm, point_own, sems.at[0]),
            pltpu.make_async_copy(outer_hbm.at[2 - 2 * odd_pair()], outer_own, sems.at[1]),
        ]
        for copy in copies:
            copy.start()
        odd = odd_position()
        at = quarter_rows(0, size).start + size - LATE
        bottom_ref[...] = gelu(x_ref[pl.ds(pl.multiple_of(at, LATE), LATE), :].astype(F32)).astype(BF16)
        total = jnp.concatenate([dot(before_ref[...], taps_ref[2 * odd]), dot(bottom_ref[...], taps_ref[2 * odd])], axis=0)
        act1_ref[...] = gelu(x_ref[quarter_rows(1, size), :].astype(F32)).astype(BF16)
        total = total + dot(act1_ref[...], taps_ref[1])
        act2_ref[...] = gelu(x_ref[quarter_rows(2, size), :].astype(F32)).astype(BF16)
        total = total + dot(act2_ref[...], taps_ref[2 - 2 * odd])
        mid = gelu(total + bias_conv_ref[...]).astype(BF16)
        copies[0].wait()
        one = x_ref[quarter_rows(1, size), :].astype(F32) + dot(mid, point_own[...]) + bias_point_ref[...]
        one = one.astype(BF16)
        one_ref[...] = one
        far = gelu(one.astype(F32)).astype(BF16)
        far_ref[...] = far
        copies[1].wait()
        second_ref[...] = dot(far, outer_own[...]).astype(BF16)

    point, outer = (pltpu.with_memory_space_constraint(w, pltpu.HBM) for w in (point, outer))
    args = (x, act, taps, bias_conv, point, bias_point, outer)
    return call(
        body, "layer1", [shape(LATE, c)] + [shape(size, c)] * 4 + [shape(size, m)], args, 10 * size * c * m,
        [pltpu.VMEM((m, c), BF16), pltpu.VMEM((c, m), BF16), pltpu.SemaphoreType.DMA((2,))],
        specs=[VMEM] * 4 + [HBM, VMEM, HBM],
    )


def after_total(total, x, point, bias_point, outer, one_ref, act_ref, product_refs):
    mid = gelu(total).astype(BF16)
    one = (x.astype(F32) + dot(mid, point[...]) + bias_point[...]).astype(BF16)
    one_ref[...] = one
    act = gelu(one.astype(F32)).astype(BF16)
    act_ref[...] = act
    odd = odd_pair()
    for tap, pieces in zip((2 * odd, 2 - 2 * odd), product_refs):
        product = dot(act, outer[tap]).astype(BF16)
        at = 0
        for ref in pieces:
            ref[...] = product[at : at + ref.shape[0], :]
            at += ref.shape[0]


def layer(x, quarter, acts, arrived, weights, pieces):
    taps, bias_conv, point, bias_point, outer = weights
    size, (c, m) = x.shape[0] // 4, taps.shape[1:]
    given = [a for a in acts if a is not None]
    known = [a is not None for a in acts]
    n = len(pieces)

    def body(*refs):
        refs = list(refs)
        x_ref = refs.pop(0)
        sources = [refs.pop(0) if k else None for k in known]
        arrived_refs = [refs.pop(0) for _ in arrived]
        taps_ref, bias_conv_ref, point_ref, bias_point_ref, outer_ref = refs[:5]
        refs = refs[5:]
        one_ref, act_ref = refs[:2]
        product_refs = refs[2 : 2 + n], refs[2 + n : 2 + 2 * n]
        x_own, sem = refs[2 + 2 * n :]
        odd = odd_position()
        copy = pltpu.make_async_copy(x_ref.at[quarter_rows(quarter, size)], x_own, sem)
        copy.start()
        total = None
        for k, source in enumerate(sources):
            if source is not None:
                term = dot(source[...], taps_ref[k + odd * (2 - 2 * k)])
                total = term if total is None else total + term
        if arrived:
            parts, missing = [], size
            for ref, (_, first) in zip(arrived_refs, arrived):
                rows = min(ref.shape[0] - first, missing)
                parts.append(ref[first : first + rows, :].astype(F32))
                missing -= rows
            total = total + (parts[0] if len(parts) == 1 else jnp.concatenate(parts, axis=0))
        copy.wait()
        after_total(
            total + bias_conv_ref[...], x_own[...], point_ref, bias_point_ref, outer_ref, one_ref, act_ref, product_refs
        )

    args = [x] + given + [value for value, _ in arrived] + list(weights)
    outs = [shape(size, c)] * 2 + [shape(rows, m) for rows in pieces] * 2
    results = call(
        body, f"layer{quarter}", outs, args, 12 * size * c * m,
        [pltpu.VMEM((size, c), BF16), pltpu.SemaphoreType.DMA],
        specs=[HBM] + [VMEM] * (len(args) - 1),
    )
    return *results[: -2 * n], list(zip(results[-2 * n : -n], results[-n:]))


def centre(acts, outer, bias_conv):
    size, c = acts[0].shape
    m = outer.shape[2]
    n = len(acts)

    def body(*refs):
        outer_ref, bias_ref = refs[n : n + 2]
        for act_ref, out_ref in zip(refs[:n], refs[n + 2 :]):
            out_ref[...] = dot(act_ref[...], outer_ref[1]) + bias_ref[...]

    args = list(acts) + [outer, bias_conv]
    return call(body, "centre", [shape(size, m, F32)] * n, args, 2 * n * size * c * m, [], specs=[VMEM] * len(args))


def finish(quarter, at, centre_sum, one_side, other_side, one, point, bias_point, whole):
    size, c = one.shape
    rows, m = one_side.shape
    steps = 2 if rows % 256 == 0 else 1
    step = rows // steps

    def body(centre_ref, one_side_ref, other_side_ref, one_ref, point_ref, bias_ref, *rest):
        out_hbm, held, sems = rest[-3:]
        start = quarter_rows(quarter, size).start + at
        copies = []
        for k in range(steps):
            part, own = pl.ds(k * step, step), pl.ds(at + k * step, step)
            total = centre_ref[own, :] + one_side_ref[part, :].astype(F32) + other_side_ref[part, :].astype(F32)
            mid = gelu(total).astype(BF16)
            out = one_ref[own, :].astype(F32) + dot(mid, point_ref[...]) + bias_ref[...]
            held[k] = out.astype(BF16)
            to = pl.ds(pl.multiple_of(start + k * step, 128), step)
            copies.append(pltpu.make_async_copy(held.at[k], out_hbm.at[to], sems.at[k]))
            copies[k].start()
        for copy in copies:
            copy.wait()

    args = [centre_sum, one_side, other_side, one, point, bias_point] + ([] if whole is None else [whole])
    return call(
        body, f"finish{quarter}", [shape(4 * size, c)], args, 2 * rows * c * m,
        [pltpu.VMEM((steps, step, c), BF16), pltpu.SemaphoreType.DMA((steps,))],
        aliases={} if whole is None else {6: 0}, out_specs=[ANY], specs=[VMEM] * 6 + [ANY] * (len(args) - 6),
    )[0]


def per_device(
    tower_input,
    first_conv_taps,
    first_conv_bias,
    first_point_weight,
    first_point_bias,
    second_conv_taps,
    second_conv_bias,
    second_point_weight,
    second_point_bias,
):
    size = tower_input.shape[0] // 4
    whole = (size,)
    split = (size - LAST_PIECE, LAST_PIECE)

    near = (first_conv_taps, first_conv_bias[None, :], first_point_weight, first_point_bias[None, :], second_conv_taps)
    x = pltpu.with_memory_space_constraint(tower_input, pltpu.HBM)
    rim_taps = pltpu.with_memory_space_constraint(first_conv_taps, pltpu.HBM)

    def to_partner(value):
        return swap(value, lambda i: i % 2 == 0, 1)

    def second_matching(value):
        return swap(value, lambda i: i // 2 % 2 == 1, 2)

    def first_matching(value):
        return swap(value, lambda i: i // 2 % 2 == 0, 2)

    def send(products):
        return [(second_matching(second), first_matching(first)) for first, second in products]

    act_top, direct = rim(x, rim_taps, 0, size - LATE)
    from_pair = swap(direct, lambda i: i % 2 == 1, 1)
    act_bottom, act1, act2, one1, far1, second1 = first_quarter(tower_input, act_top, near)
    far1, second1 = lax.optimization_barrier((far1, second1))
    side1 = second_matching(second1)
    first1, late, act0 = behind_first(far1, second_conv_taps, act_top, act_bottom, first_conv_taps)
    later, first1, late = lax.optimization_barrier((x, first1, late))
    from_pair_late = swap(late, lambda i: i % 2 == 1, 1)
    sides1 = [(side1, first_matching(first1))]
    act3, for_partner = rim(later, rim_taps, 3, size)
    from_partner = to_partner(for_partner)
    one2, far2, products2 = layer(x, 2, (act1, act2, act3), [], near, whole)
    sides2 = send(products2)
    one0, far0, products0 = layer(
        x, 0, (None, act0, act1), [(from_pair, 0), (from_pair_late, 0)], near, whole
    )
    sides0 = send(products0)
    one3, far3, products3 = layer(x, 3, (act2, act3, None), [(from_partner, 0)], near, split)
    sides3 = send(products3)

    centres = centre((far1, far2, far0, far3), second_conv_taps, second_conv_bias[None, :])
    out = None
    for quarter, total, sides, one in zip(
        (1, 2, 0, 3), centres, (sides1, sides2, sides0, sides3), (one1, one2, one0, one3)
    ):
        at = 0
        for pair in sides:
            out = finish(quarter, at, total, *pair, one, second_point_weight, second_point_bias[None, :], out)
            at += pair[0].shape[0]
    return out


def solution(mesh):
    return jax.shard_map(
        per_device,
        mesh=mesh,
        in_specs=(P(("grp", "seq"), None), P(), P(), P(), P(), P(), P(), P(), P()),
        out_specs=P(("grp", "seq"), None),
        check_vma=False,
    )
```

```python
import math

import jax
import jax.numpy as jnp
from jax import lax
from jax.experimental import pallas as pl
from jax.experimental.pallas import tpu as pltpu
from jax.sharding import PartitionSpec as P

LIMIT = 16 * 1024 * 1024
VMEM = pl.BlockSpec(memory_space=pltpu.VMEM)
ANY = pl.BlockSpec(memory_space=pl.ANY)
HBM = pl.BlockSpec(memory_space=pltpu.HBM)
SLOPE = math.sqrt(2.0 / math.pi)
LAST_PIECE = 160
BF16 = jnp.bfloat16
F32 = jnp.float32


def swap(value, first, step):
    size = lax.axis_size("seq")
    pairs = []
    for i in range(size):
        if first(i):
            j = (i + step) % size
            pairs += [(i, j), (j, i)]
    return lax.ppermute(value, "seq", sorted(pairs))


def gelu(v):
    half = 0.5 * v
    return half + half * jnp.tanh(v * (SLOPE + (SLOPE * 0.044715) * (v * v)))


def dot(a, b):
    return jnp.dot(a, b, preferred_element_type=F32)


def odd_position():
    return lax.rem(lax.axis_index("seq"), 2)


def quarter_rows(quarter, size):
    at = quarter + odd_position() * (3 - 2 * quarter)
    return pl.ds(pl.multiple_of(at * size, size), size)


def call(body, name, out_shape, args, flops, scratch, aliases=None, out_specs=None, specs=None):
    moved = sum(a.size * a.dtype.itemsize for a in args)
    return pl.pallas_call(
        body,
        in_specs=specs,
        out_specs=[VMEM] * len(out_shape) if out_specs is None else out_specs,
        out_shape=out_shape,
        scratch_shapes=scratch,
        input_output_aliases=aliases or {},
        compiler_params=pltpu.CompilerParams(vmem_limit_bytes=LIMIT),
        cost_estimate=pl.CostEstimate(flops=flops, bytes_accessed=moved, transcendentals=0),
        name=name,
    )(*args)


def shape(rows, columns, dtype=BF16):
    return jax.ShapeDtypeStruct((rows, columns), dtype)


def rim_activations(x_ref, taps_ref, tap, quarter, size, act_ref, product_ref, x_own, tap_own, sems):
    rows = x_own.shape[0]
    half = size // 2
    top, bottom = pl.ds(0, half), pl.ds(half, rows - half)
    which = tap + odd_position() * (2 - 2 * tap)
    start = quarter_rows(quarter, size).start
    copies = [
        pltpu.make_async_copy(x_ref.at[pl.ds(pl.multiple_of(start, half), half)], x_own.at[top], sems.at[0]),
        pltpu.make_async_copy(taps_ref.at[which], tap_own, sems.at[1]),
        pltpu.make_async_copy(
            x_ref.at[pl.ds(pl.multiple_of(start + half, half), rows - half)], x_own.at[bottom], sems.at[2]
        ),
    ]
    for copy in copies:
        copy.start()
    copies[0].wait()
    act_ref[top, :] = gelu(x_own[top, :].astype(F32)).astype(BF16)
    copies[1].wait()
    copies[2].wait()
    product_ref[top, :] = dot(act_ref[top, :], tap_own[...]).astype(BF16)
    act_ref[bottom, :] = gelu(x_own[bottom, :].astype(F32)).astype(BF16)
    product_ref[bottom, :] = dot(act_ref[bottom, :], tap_own[...]).astype(BF16)


def rim(x, taps, quarter, rows):
    size, (c, m) = x.shape[0] // 4, taps.shape[1:]

    def body(x_ref, taps_ref, act_ref, product_ref, *scratch):
        tap = 2 if quarter == 0 else 0
        rim_activations(x_ref, taps_ref, tap, quarter, size, act_ref, product_ref, *scratch)

    return call(
        body, f"rim{quarter}", [shape(rows, c), shape(rows, m)], (x, taps), 2 * rows * c * m,
        [pltpu.VMEM((rows, c), BF16), pltpu.VMEM((c, m), BF16), pltpu.SemaphoreType.DMA((3,))], specs=[HBM] * 2,
    )


def odd_pair():
    return lax.rem(lax.div(lax.axis_index("seq"), 2), 2)


def first_quarter(x, act, weights):
    taps, bias_conv, point, bias_point, outer = weights
    size, (c, m) = x.shape[0] // 4, taps.shape[1:]

    def body(
        x_ref, before_ref, taps_ref, bias_conv_ref, point_hbm, bias_point_ref, outer_hbm,
        act1_ref, act2_ref, one_ref, far_ref, first_ref, second_ref, point_own, outer_own, sems,
    ):
        copies = [
            pltpu.make_async_copy(point_hbm, point_own, sems.at[0]),
            pltpu.make_async_copy(outer_hbm.at[2 - 2 * odd_pair()], outer_own.at[1], sems.at[1]),
            pltpu.make_async_copy(outer_hbm.at[2 * odd_pair()], outer_own.at[0], sems.at[2]),
        ]
        for copy in copies:
            copy.start()
        odd = odd_position()
        total = dot(before_ref[...], taps_ref[2 * odd])
        act1_ref[...] = gelu(x_ref[quarter_rows(1, size), :].astype(F32)).astype(BF16)
        total = total + dot(act1_ref[...], taps_ref[1])
        act2_ref[...] = gelu(x_ref[quarter_rows(2, size), :].astype(F32)).astype(BF16)
        total = total + dot(act2_ref[...], taps_ref[2 - 2 * odd])
        mid = gelu(total + bias_conv_ref[...]).astype(BF16)
        copies[0].wait()
        one = x_ref[quarter_rows(1, size), :].astype(F32) + dot(mid, point_own[...]) + bias_point_ref[...]
        one = one.astype(BF16)
        one_ref[...] = one
        far = gelu(one.astype(F32)).astype(BF16)
        far_ref[...] = far
        copies[1].wait()
        second_ref[...] = dot(far, outer_own[1]).astype(BF16)
        copies[2].wait()
        first_ref[...] = dot(far, outer_own[0]).astype(BF16)

    point, outer = (pltpu.with_memory_space_constraint(w, pltpu.HBM) for w in (point, outer))
    args = (x, act, taps, bias_conv, point, bias_point, outer)
    return call(
        body, "layer1", [shape(size, c)] * 4 + [shape(size, m)] * 2, args, 12 * size * c * m,
        [pltpu.VMEM((m, c), BF16), pltpu.VMEM((2, c, m), BF16), pltpu.SemaphoreType.DMA((3,))],
        specs=[VMEM] * 4 + [HBM, VMEM, HBM],
    )


def after_total(total, x, point, bias_point, outer, one_ref, act_ref, product_refs):
    mid = gelu(total).astype(BF16)
    one = (x.astype(F32) + dot(mid, point[...]) + bias_point[...]).astype(BF16)
    one_ref[...] = one
    act = gelu(one.astype(F32)).astype(BF16)
    act_ref[...] = act
    odd = odd_pair()
    for tap, pieces in zip((2 * odd, 2 - 2 * odd), product_refs):
        product = dot(act, outer[tap]).astype(BF16)
        at = 0
        for ref in pieces:
            ref[...] = product[at : at + ref.shape[0], :]
            at += ref.shape[0]


def layer(x, quarter, acts, arrived, weights, pieces):
    taps, bias_conv, point, bias_point, outer = weights
    size, (c, m) = x.shape[0] // 4, taps.shape[1:]
    given = [a for a in acts if a is not None]
    known = [a is not None for a in acts]
    n = len(pieces)

    def body(*refs):
        refs = list(refs)
        x_ref = refs.pop(0)
        sources = [refs.pop(0) if k else None for k in known]
        arrived_refs = [refs.pop(0) for _ in arrived]
        taps_ref, bias_conv_ref, point_ref, bias_point_ref, outer_ref = refs[:5]
        refs = refs[5:]
        one_ref, act_ref = refs[:2]
        product_refs = refs[2 : 2 + n], refs[2 + n : 2 + 2 * n]
        x_own, sem = refs[2 + 2 * n :]
        odd = odd_position()
        copy = pltpu.make_async_copy(x_ref.at[quarter_rows(quarter, size)], x_own, sem)
        copy.start()
        total = None
        for k, source in enumerate(sources):
            if source is not None:
                term = dot(source[...], taps_ref[k + odd * (2 - 2 * k)])
                total = term if total is None else total + term
        if arrived:
            parts, missing = [], size
            for ref, (_, first) in zip(arrived_refs, arrived):
                rows = min(ref.shape[0] - first, missing)
                parts.append(ref[first : first + rows, :].astype(F32))
                missing -= rows
            total = total + (parts[0] if len(parts) == 1 else jnp.concatenate(parts, axis=0))
        copy.wait()
        after_total(
            total + bias_conv_ref[...], x_own[...], point_ref, bias_point_ref, outer_ref, one_ref, act_ref, product_refs
        )

    args = [x] + given + [value for value, _ in arrived] + list(weights)
    outs = [shape(size, c)] * 2 + [shape(rows, m) for rows in pieces] * 2
    results = call(
        body, f"layer{quarter}", outs, args, 12 * size * c * m,
        [pltpu.VMEM((size, c), BF16), pltpu.SemaphoreType.DMA],
        specs=[HBM] + [VMEM] * (len(args) - 1),
    )
    return *results[: -2 * n], list(zip(results[-2 * n : -n], results[-n:]))


def centre(acts, outer, bias_conv):
    size, c = acts[0].shape
    m = outer.shape[2]
    n = len(acts)

    def body(*refs):
        outer_ref, bias_ref = refs[n : n + 2]
        for act_ref, out_ref in zip(refs[:n], refs[n + 2 :]):
            out_ref[...] = dot(act_ref[...], outer_ref[1]) + bias_ref[...]

    args = list(acts) + [outer, bias_conv]
    return call(body, "centre", [shape(size, m, F32)] * n, args, 2 * n * size * c * m, [], specs=[VMEM] * len(args))


def finish(quarter, at, centre_sum, one_side, other_side, one, point, bias_point, whole):
    size, c = one.shape
    rows, m = one_side.shape
    steps = 2 if rows % 256 == 0 else 1
    step = rows // steps

    def body(centre_ref, one_side_ref, other_side_ref, one_ref, point_ref, bias_ref, *rest):
        out_hbm, held, sems = rest[-3:]
        start = quarter_rows(quarter, size).start + at
        copies = []
        for k in range(steps):
            part, own = pl.ds(k * step, step), pl.ds(at + k * step, step)
            total = centre_ref[own, :] + one_side_ref[part, :].astype(F32) + other_side_ref[part, :].astype(F32)
            mid = gelu(total).astype(BF16)
            out = one_ref[own, :].astype(F32) + dot(mid, point_ref[...]) + bias_ref[...]
            held[k] = out.astype(BF16)
            to = pl.ds(pl.multiple_of(start + k * step, 32), step)
            copies.append(pltpu.make_async_copy(held.at[k], out_hbm.at[to], sems.at[k]))
            copies[k].start()
        for copy in copies:
            copy.wait()

    args = [centre_sum, one_side, other_side, one, point, bias_point] + ([] if whole is None else [whole])
    return call(
        body, f"finish{quarter}", [shape(4 * size, c)], args, 2 * rows * c * m,
        [pltpu.VMEM((steps, step, c), BF16), pltpu.SemaphoreType.DMA((steps,))],
        aliases={} if whole is None else {6: 0}, out_specs=[ANY], specs=[VMEM] * 6 + [ANY] * (len(args) - 6),
    )[0]


def per_device(
    tower_input,
    first_conv_taps,
    first_conv_bias,
    first_point_weight,
    first_point_bias,
    second_conv_taps,
    second_conv_bias,
    second_point_weight,
    second_point_bias,
):
    size = tower_input.shape[0] // 4
    whole = (size,)
    split = (size - LAST_PIECE, LAST_PIECE)

    near = (first_conv_taps, first_conv_bias[None, :], first_point_weight, first_point_bias[None, :], second_conv_taps)
    x = pltpu.with_memory_space_constraint(tower_input, pltpu.HBM)
    rim_taps = pltpu.with_memory_space_constraint(first_conv_taps, pltpu.HBM)

    def to_partner(value):
        return swap(value, lambda i: i % 2 == 0, 1)

    def second_matching(value):
        return swap(value, lambda i: i // 2 % 2 == 1, 2)

    def first_matching(value):
        return swap(value, lambda i: i // 2 % 2 == 0, 2)

    def send(products):
        return [(second_matching(second), first_matching(first)) for first, second in products]

    act0, to_pair = rim(x, rim_taps, 0, size)
    from_pair = swap(to_pair, lambda i: i % 2 == 1, 1)
    act1, act2, one1, far1, *products1 = first_quarter(tower_input, act0, near)
    later, products1 = lax.optimization_barrier((x, products1))
    sides1 = send([products1])
    act3, for_partner = rim(later, rim_taps, 3, size)
    from_partner = to_partner(for_partner)
    one2, far2, products2 = layer(x, 2, (act1, act2, act3), [], near, whole)
    sides2 = send(products2)
    one0, far0, products0 = layer(
        x, 0, (None, act0, act1), [(from_pair, 0)], near, whole
    )
    sides0 = send(products0)
    one3, far3, products3 = layer(x, 3, (act2, act3, None), [(from_partner, 0)], near, split)
    sides3 = send(products3)

    centres = centre((far1, far2, far0, far3), second_conv_taps, second_conv_bias[None, :])
    out = None
    for quarter, total, sides, one in zip(
        (1, 2, 0, 3), centres, (sides1, sides2, sides0, sides3), (one1, one2, one0, one3)
    ):
        at = 0
        for pair in sides:
            out = finish(quarter, at, total, *pair, one, second_point_weight, second_point_bias[None, :], out)
            at += pair[0].shape[0]
    return out


def solution(mesh):
    return jax.shard_map(
        per_device,
        mesh=mesh,
        in_specs=(P(("grp", "seq"), None), P(), P(), P(), P(), P(), P(), P(), P()),
        out_specs=P(("grp", "seq"), None),
        check_vma=False,
    )
```

```python
import math

import jax
import jax.numpy as jnp
from jax import lax
from jax.experimental import pallas as pl
from jax.experimental.pallas import tpu as pltpu
from jax.sharding import PartitionSpec as P

LIMIT = 16 * 1024 * 1024
VMEM = pl.BlockSpec(memory_space=pltpu.VMEM)
ANY = pl.BlockSpec(memory_space=pl.ANY)
HBM = pl.BlockSpec(memory_space=pltpu.HBM)
SLOPE = math.sqrt(2.0 / math.pi)
LAST_PIECE = 128
BF16 = jnp.bfloat16
F32 = jnp.float32


def swap(value, first, step):
    size = lax.axis_size("seq")
    pairs = []
    for i in range(size):
        if first(i):
            j = (i + step) % size
            pairs += [(i, j), (j, i)]
    return lax.ppermute(value, "seq", sorted(pairs))


def gelu(v):
    half = 0.5 * v
    return half + half * jnp.tanh(v * (SLOPE + (SLOPE * 0.044715) * (v * v)))


def dot(a, b):
    return jnp.dot(a, b, preferred_element_type=F32)


def odd_position():
    return lax.rem(lax.axis_index("seq"), 2)


def quarter_rows(quarter, size):
    at = quarter + odd_position() * (3 - 2 * quarter)
    return pl.ds(pl.multiple_of(at * size, size), size)


def call(body, name, out_shape, args, flops, scratch, aliases=None, out_specs=None, specs=None):
    moved = sum(a.size * a.dtype.itemsize for a in args)
    return pl.pallas_call(
        body,
        in_specs=specs,
        out_specs=[VMEM] * len(out_shape) if out_specs is None else out_specs,
        out_shape=out_shape,
        scratch_shapes=scratch,
        input_output_aliases=aliases or {},
        compiler_params=pltpu.CompilerParams(vmem_limit_bytes=LIMIT),
        cost_estimate=pl.CostEstimate(flops=flops, bytes_accessed=moved, transcendentals=0),
        name=name,
    )(*args)


def shape(rows, columns, dtype=BF16):
    return jax.ShapeDtypeStruct((rows, columns), dtype)


def rim_activations(x_ref, taps_ref, tap, quarter, size, act_ref, product_ref, x_own, tap_own, sems):
    rows = x_own.shape[0]
    half = size // 2
    top, bottom = pl.ds(0, half), pl.ds(half, rows - half)
    which = tap + odd_position() * (2 - 2 * tap)
    start = quarter_rows(quarter, size).start
    copies = [
        pltpu.make_async_copy(x_ref.at[pl.ds(pl.multiple_of(start, half), half)], x_own.at[top], sems.at[0]),
        pltpu.make_async_copy(taps_ref.at[which], tap_own, sems.at[1]),
        pltpu.make_async_copy(
            x_ref.at[pl.ds(pl.multiple_of(start + half, half), rows - half)], x_own.at[bottom], sems.at[2]
        ),
    ]
    for copy in copies:
        copy.start()
    copies[0].wait()
    act_ref[top, :] = gelu(x_own[top, :].astype(F32)).astype(BF16)
    copies[1].wait()
    copies[2].wait()
    product_ref[top, :] = dot(act_ref[top, :], tap_own[...]).astype(BF16)
    act_ref[bottom, :] = gelu(x_own[bottom, :].astype(F32)).astype(BF16)
    product_ref[bottom, :] = dot(act_ref[bottom, :], tap_own[...]).astype(BF16)


def rim(x, taps, quarter, rows):
    size, (c, m) = x.shape[0] // 4, taps.shape[1:]

    def body(x_ref, taps_ref, act_ref, product_ref, *scratch):
        tap = 2 if quarter == 0 else 0
        rim_activations(x_ref, taps_ref, tap, quarter, size, act_ref, product_ref, *scratch)

    return call(
        body, f"rim{quarter}", [shape(rows, c), shape(rows, m)], (x, taps), 2 * rows * c * m,
        [pltpu.VMEM((rows, c), BF16), pltpu.VMEM((c, m), BF16), pltpu.SemaphoreType.DMA((3,))], specs=[HBM] * 2,
    )


def odd_pair():
    return lax.rem(lax.div(lax.axis_index("seq"), 2), 2)


def first_quarter(x, act, weights):
    taps, bias_conv, point, bias_point, outer = weights
    size, (c, m) = x.shape[0] // 4, taps.shape[1:]

    def body(
        x_ref, before_ref, taps_ref, bias_conv_ref, point_hbm, bias_point_ref, outer_hbm,
        act1_ref, act2_ref, one_ref, far_ref, first_ref, second_ref, point_own, outer_own, sems,
    ):
        copies = [
            pltpu.make_async_copy(point_hbm, point_own, sems.at[0]),
            pltpu.make_async_copy(outer_hbm.at[2 - 2 * odd_pair()], outer_own.at[1], sems.at[1]),
            pltpu.make_async_copy(outer_hbm.at[2 * odd_pair()], outer_own.at[0], sems.at[2]),
        ]
        for copy in copies:
            copy.start()
        odd = odd_position()
        total = dot(before_ref[...], taps_ref[2 * odd])
        act1_ref[...] = gelu(x_ref[quarter_rows(1, size), :].astype(F32)).astype(BF16)
        total = total + dot(act1_ref[...], taps_ref[1])
        act2_ref[...] = gelu(x_ref[quarter_rows(2, size), :].astype(F32)).astype(BF16)
        total = total + dot(act2_ref[...], taps_ref[2 - 2 * odd])
        mid = gelu(total + bias_conv_ref[...]).astype(BF16)
        copies[0].wait()
        one = x_ref[quarter_rows(1, size), :].astype(F32) + dot(mid, point_own[...]) + bias_point_ref[...]
        one = one.astype(BF16)
        one_ref[...] = one
        far = gelu(one.astype(F32)).astype(BF16)
        far_ref[...] = far
        copies[1].wait()
        second_ref[...] = dot(far, outer_own[1]).astype(BF16)
        copies[2].wait()
        first_ref[...] = dot(far, outer_own[0]).astype(BF16)

    point, outer = (pltpu.with_memory_space_constraint(w, pltpu.HBM) for w in (point, outer))
    args = (x, act, taps, bias_conv, point, bias_point, outer)
    return call(
        body, "layer1", [shape(size, c)] * 4 + [shape(size, m)] * 2, args, 12 * size * c * m,
        [pltpu.VMEM((m, c), BF16), pltpu.VMEM((2, c, m), BF16), pltpu.SemaphoreType.DMA((3,))],
        specs=[VMEM] * 4 + [HBM, VMEM, HBM],
    )


def after_total(total, x, point, bias_point, outer, one_ref, act_ref, product_refs):
    mid = gelu(total).astype(BF16)
    one = (x.astype(F32) + dot(mid, point[...]) + bias_point[...]).astype(BF16)
    one_ref[...] = one
    act = gelu(one.astype(F32)).astype(BF16)
    act_ref[...] = act
    odd = odd_pair()
    for tap, pieces in zip((2 * odd, 2 - 2 * odd), product_refs):
        product = dot(act, outer[tap]).astype(BF16)
        at = 0
        for ref in pieces:
            ref[...] = product[at : at + ref.shape[0], :]
            at += ref.shape[0]


def layer(x, quarter, acts, arrived, weights, pieces):
    taps, bias_conv, point, bias_point, outer = weights
    size, (c, m) = x.shape[0] // 4, taps.shape[1:]
    given = [a for a in acts if a is not None]
    known = [a is not None for a in acts]
    n = len(pieces)

    def body(*refs):
        refs = list(refs)
        x_ref = refs.pop(0)
        sources = [refs.pop(0) if k else None for k in known]
        arrived_refs = [refs.pop(0) for _ in arrived]
        taps_ref, bias_conv_ref, point_ref, bias_point_ref, outer_ref = refs[:5]
        refs = refs[5:]
        one_ref, act_ref = refs[:2]
        product_refs = refs[2 : 2 + n], refs[2 + n : 2 + 2 * n]
        x_own, sem = refs[2 + 2 * n :]
        odd = odd_position()
        copy = pltpu.make_async_copy(x_ref.at[quarter_rows(quarter, size)], x_own, sem)
        copy.start()
        total = None
        for k, source in enumerate(sources):
            if source is not None:
                term = dot(source[...], taps_ref[k + odd * (2 - 2 * k)])
                total = term if total is None else total + term
        if arrived:
            parts, missing = [], size
            for ref, (_, first) in zip(arrived_refs, arrived):
                rows = min(ref.shape[0] - first, missing)
                parts.append(ref[first : first + rows, :].astype(F32))
                missing -= rows
            total = total + (parts[0] if len(parts) == 1 else jnp.concatenate(parts, axis=0))
        copy.wait()
        after_total(
            total + bias_conv_ref[...], x_own[...], point_ref, bias_point_ref, outer_ref, one_ref, act_ref, product_refs
        )

    args = [x] + given + [value for value, _ in arrived] + list(weights)
    outs = [shape(size, c)] * 2 + [shape(rows, m) for rows in pieces] * 2
    results = call(
        body, f"layer{quarter}", outs, args, 12 * size * c * m,
        [pltpu.VMEM((size, c), BF16), pltpu.SemaphoreType.DMA],
        specs=[HBM] + [VMEM] * (len(args) - 1),
    )
    return *results[: -2 * n], list(zip(results[-2 * n : -n], results[-n:]))


def centre(acts, outer, bias_conv):
    size, c = acts[0].shape
    m = outer.shape[2]
    n = len(acts)

    def body(*refs):
        outer_ref, bias_ref = refs[n : n + 2]
        for act_ref, out_ref in zip(refs[:n], refs[n + 2 :]):
            out_ref[...] = dot(act_ref[...], outer_ref[1]) + bias_ref[...]

    args = list(acts) + [outer, bias_conv]
    return call(body, "centre", [shape(size, m, F32)] * n, args, 2 * n * size * c * m, [], specs=[VMEM] * len(args))


def finish(quarter, at, centre_sum, one_side, other_side, one, point, bias_point, whole):
    size, c = one.shape
    rows, m = one_side.shape
    steps = 2 if rows % 256 == 0 else 1
    step = rows // steps

    def body(centre_ref, one_side_ref, other_side_ref, one_ref, point_ref, bias_ref, *rest):
        out_hbm, held, sems = rest[-3:]
        start = quarter_rows(quarter, size).start + at
        copies = []
        for k in range(steps):
            part, own = pl.ds(k * step, step), pl.ds(at + k * step, step)
            total = centre_ref[own, :] + one_side_ref[part, :].astype(F32) + other_side_ref[part, :].astype(F32)
            mid = gelu(total).astype(BF16)
            out = one_ref[own, :].astype(F32) + dot(mid, point_ref[...]) + bias_ref[...]
            held[k] = out.astype(BF16)
            to = pl.ds(pl.multiple_of(start + k * step, 32), step)
            copies.append(pltpu.make_async_copy(held.at[k], out_hbm.at[to], sems.at[k]))
            copies[k].start()
        for copy in copies:
            copy.wait()

    args = [centre_sum, one_side, other_side, one, point, bias_point] + ([] if whole is None else [whole])
    return call(
        body, f"finish{quarter}", [shape(4 * size, c)], args, 2 * rows * c * m,
        [pltpu.VMEM((steps, step, c), BF16), pltpu.SemaphoreType.DMA((steps,))],
        aliases={} if whole is None else {6: 0}, out_specs=[ANY], specs=[VMEM] * 6 + [ANY] * (len(args) - 6),
    )[0]


def per_device(
    tower_input,
    first_conv_taps,
    first_conv_bias,
    first_point_weight,
    first_point_bias,
    second_conv_taps,
    second_conv_bias,
    second_point_weight,
    second_point_bias,
):
    size = tower_input.shape[0] // 4
    whole = (size,)
    split = (size - LAST_PIECE, LAST_PIECE)

    near = (first_conv_taps, first_conv_bias[None, :], first_point_weight, first_point_bias[None, :], second_conv_taps)
    x = pltpu.with_memory_space_constraint(tower_input, pltpu.HBM)
    rim_taps = pltpu.with_memory_space_constraint(first_conv_taps, pltpu.HBM)

    def to_partner(value):
        return swap(value, lambda i: i % 2 == 0, 1)

    def second_matching(value):
        return swap(value, lambda i: i // 2 % 2 == 1, 2)

    def first_matching(value):
        return swap(value, lambda i: i // 2 % 2 == 0, 2)

    def send(products):
        return [(second_matching(second), first_matching(first)) for first, second in products]

    act0, to_pair = rim(x, rim_taps, 0, size)
    from_pair = swap(to_pair, lambda i: i % 2 == 1, 1)
    act1, act2, one1, far1, *products1 = first_quarter(tower_input, act0, near)
    later, products1 = lax.optimization_barrier((x, products1))
    sides1 = send([products1])
    act3, for_partner = rim(later, rim_taps, 3, size)
    from_partner = to_partner(for_partner)
    one2, far2, products2 = layer(x, 2, (act1, act2, act3), [], near, whole)
    sides2 = send(products2)
    one0, far0, products0 = layer(
        x, 0, (None, act0, act1), [(from_pair, 0)], near, whole
    )
    sides0 = send(products0)
    one3, far3, products3 = layer(x, 3, (act2, act3, None), [(from_partner, 0)], near, split)
    sides3 = send(products3)

    centres = centre((far1, far2, far0, far3), second_conv_taps, second_conv_bias[None, :])
    out = None
    for quarter, total, sides, one in zip(
        (1, 2, 0, 3), centres, (sides1, sides2, sides0, sides3), (one1, one2, one0, one3)
    ):
        at = 0
        for pair in sides:
            out = finish(quarter, at, total, *pair, one, second_point_weight, second_point_bias[None, :], out)
            at += pair[0].shape[0]
    return out


def solution(mesh):
    return jax.shard_map(
        per_device,
        mesh=mesh,
        in_specs=(P(("grp", "seq"), None), P(), P(), P(), P(), P(), P(), P(), P()),
        out_specs=P(("grp", "seq"), None),
        check_vma=False,
    )
```

```python
import math

import jax
import jax.numpy as jnp
from jax import lax
from jax.experimental import pallas as pl
from jax.experimental.pallas import tpu as pltpu
from jax.sharding import PartitionSpec as P

LIMIT = 16 * 1024 * 1024
VMEM = pl.BlockSpec(memory_space=pltpu.VMEM)
ANY = pl.BlockSpec(memory_space=pl.ANY)
HBM = pl.BlockSpec(memory_space=pltpu.HBM)
SLOPE = math.sqrt(2.0 / math.pi)
LAST_PIECE = 96
BF16 = jnp.bfloat16
F32 = jnp.float32


def swap(value, first, step):
    size = lax.axis_size("seq")
    pairs = []
    for i in range(size):
        if first(i):
            j = (i + step) % size
            pairs += [(i, j), (j, i)]
    return lax.ppermute(value, "seq", sorted(pairs))


def gelu(v):
    half = 0.5 * v
    return half + half * jnp.tanh(v * (SLOPE + (SLOPE * 0.044715) * (v * v)))


def dot(a, b):
    return jnp.dot(a, b, preferred_element_type=F32)


def odd_position():
    return lax.rem(lax.axis_index("seq"), 2)


def quarter_rows(quarter, size):
    at = quarter + odd_position() * (3 - 2 * quarter)
    return pl.ds(pl.multiple_of(at * size, size), size)


def call(body, name, out_shape, args, flops, scratch, aliases=None, out_specs=None, specs=None):
    moved = sum(a.size * a.dtype.itemsize for a in args)
    return pl.pallas_call(
        body,
        in_specs=specs,
        out_specs=[VMEM] * len(out_shape) if out_specs is None else out_specs,
        out_shape=out_shape,
        scratch_shapes=scratch,
        input_output_aliases=aliases or {},
        compiler_params=pltpu.CompilerParams(vmem_limit_bytes=LIMIT),
        cost_estimate=pl.CostEstimate(flops=flops, bytes_accessed=moved, transcendentals=0),
        name=name,
    )(*args)


def shape(rows, columns, dtype=BF16):
    return jax.ShapeDtypeStruct((rows, columns), dtype)


def rim_activations(x_ref, taps_ref, tap, quarter, size, act_ref, product_ref, x_own, tap_own, sems):
    rows = x_own.shape[0]
    half = size // 2
    top, bottom = pl.ds(0, half), pl.ds(half, rows - half)
    which = tap + odd_position() * (2 - 2 * tap)
    start = quarter_rows(quarter, size).start
    copies = [
        pltpu.make_async_copy(x_ref.at[pl.ds(pl.multiple_of(start, half), half)], x_own.at[top], sems.at[0]),
        pltpu.make_async_copy(taps_ref.at[which], tap_own, sems.at[1]),
        pltpu.make_async_copy(
            x_ref.at[pl.ds(pl.multiple_of(start + half, half), rows - half)], x_own.at[bottom], sems.at[2]
        ),
    ]
    for copy in copies:
        copy.start()
    copies[0].wait()
    act_ref[top, :] = gelu(x_own[top, :].astype(F32)).astype(BF16)
    copies[1].wait()
    copies[2].wait()
    product_ref[top, :] = dot(act_ref[top, :], tap_own[...]).astype(BF16)
    act_ref[bottom, :] = gelu(x_own[bottom, :].astype(F32)).astype(BF16)
    product_ref[bottom, :] = dot(act_ref[bottom, :], tap_own[...]).astype(BF16)


def rim(x, taps, quarter, rows):
    size, (c, m) = x.shape[0] // 4, taps.shape[1:]

    def body(x_ref, taps_ref, act_ref, product_ref, *scratch):
        tap = 2 if quarter == 0 else 0
        rim_activations(x_ref, taps_ref, tap, quarter, size, act_ref, product_ref, *scratch)

    return call(
        body, f"rim{quarter}", [shape(rows, c), shape(rows, m)], (x, taps), 2 * rows * c * m,
        [pltpu.VMEM((rows, c), BF16), pltpu.VMEM((c, m), BF16), pltpu.SemaphoreType.DMA((3,))], specs=[HBM] * 2,
    )


def odd_pair():
    return lax.rem(lax.div(lax.axis_index("seq"), 2), 2)


def first_quarter(x, act, weights):
    taps, bias_conv, point, bias_point, outer = weights
    size, (c, m) = x.shape[0] // 4, taps.shape[1:]

    def body(
        x_ref, before_ref, taps_ref, bias_conv_ref, point_hbm, bias_point_ref, outer_hbm,
        act1_ref, act2_ref, one_ref, far_ref, first_ref, second_ref, point_own, outer_own, sems,
    ):
        copies = [
            pltpu.make_async_copy(point_hbm, point_own, sems.at[0]),
            pltpu.make_async_copy(outer_hbm.at[2 - 2 * odd_pair()], outer_own.at[1], sems.at[1]),
            pltpu.make_async_copy(outer_hbm.at[2 * odd_pair()], outer_own.at[0], sems.at[2]),
        ]
        for copy in copies:
            copy.start()
        odd = odd_position()
        total = dot(before_ref[...], taps_ref[2 * odd])
        act1_ref[...] = gelu(x_ref[quarter_rows(1, size), :].astype(F32)).astype(BF16)
        total = total + dot(act1_ref[...], taps_ref[1])
        act2_ref[...] = gelu(x_ref[quarter_rows(2, size), :].astype(F32)).astype(BF16)
        total = total + dot(act2_ref[...], taps_ref[2 - 2 * odd])
        mid = gelu(total + bias_conv_ref[...]).astype(BF16)
        copies[0].wait()
        one = x_ref[quarter_rows(1, size), :].astype(F32) + dot(mid, point_own[...]) + bias_point_ref[...]
        one = one.astype(BF16)
        one_ref[...] = one
        far = gelu(one.astype(F32)).astype(BF16)
        far_ref[...] = far
        copies[1].wait()
        second_ref[...] = dot(far, outer_own[1]).astype(BF16)
        copies[2].wait()
        first_ref[...] = dot(far, outer_own[0]).astype(BF16)

    point, outer = (pltpu.with_memory_space_constraint(w, pltpu.HBM) for w in (point, outer))
    args = (x, act, taps, bias_conv, point, bias_point, outer)
    return call(
        body, "layer1", [shape(size, c)] * 4 + [shape(size, m)] * 2, args, 12 * size * c * m,
        [pltpu.VMEM((m, c), BF16), pltpu.VMEM((2, c, m), BF16), pltpu.SemaphoreType.DMA((3,))],
        specs=[VMEM] * 4 + [HBM, VMEM, HBM],
    )


def after_total(total, x, point, bias_point, outer, one_ref, act_ref, product_refs):
    mid = gelu(total).astype(BF16)
    one = (x.astype(F32) + dot(mid, point[...]) + bias_point[...]).astype(BF16)
    one_ref[...] = one
    act = gelu(one.astype(F32)).astype(BF16)
    act_ref[...] = act
    odd = odd_pair()
    for tap, pieces in zip((2 * odd, 2 - 2 * odd), product_refs):
        product = dot(act, outer[tap]).astype(BF16)
        at = 0
        for ref in pieces:
            ref[...] = product[at : at + ref.shape[0], :]
            at += ref.shape[0]


def layer(x, quarter, acts, arrived, weights, pieces):
    taps, bias_conv, point, bias_point, outer = weights
    size, (c, m) = x.shape[0] // 4, taps.shape[1:]
    given = [a for a in acts if a is not None]
    known = [a is not None for a in acts]
    n = len(pieces)

    def body(*refs):
        refs = list(refs)
        x_ref = refs.pop(0)
        sources = [refs.pop(0) if k else None for k in known]
        arrived_refs = [refs.pop(0) for _ in arrived]
        taps_ref, bias_conv_ref, point_ref, bias_point_ref, outer_ref = refs[:5]
        refs = refs[5:]
        one_ref, act_ref = refs[:2]
        product_refs = refs[2 : 2 + n], refs[2 + n : 2 + 2 * n]
        x_own, sem = refs[2 + 2 * n :]
        odd = odd_position()
        copy = pltpu.make_async_copy(x_ref.at[quarter_rows(quarter, size)], x_own, sem)
        copy.start()
        total = None
        for k, source in enumerate(sources):
            if source is not None:
                term = dot(source[...], taps_ref[k + odd * (2 - 2 * k)])
                total = term if total is None else total + term
        if arrived:
            parts, missing = [], size
            for ref, (_, first) in zip(arrived_refs, arrived):
                rows = min(ref.shape[0] - first, missing)
                parts.append(ref[first : first + rows, :].astype(F32))
                missing -= rows
            total = total + (parts[0] if len(parts) == 1 else jnp.concatenate(parts, axis=0))
        copy.wait()
        after_total(
            total + bias_conv_ref[...], x_own[...], point_ref, bias_point_ref, outer_ref, one_ref, act_ref, product_refs
        )

    args = [x] + given + [value for value, _ in arrived] + list(weights)
    outs = [shape(size, c)] * 2 + [shape(rows, m) for rows in pieces] * 2
    results = call(
        body, f"layer{quarter}", outs, args, 12 * size * c * m,
        [pltpu.VMEM((size, c), BF16), pltpu.SemaphoreType.DMA],
        specs=[HBM] + [VMEM] * (len(args) - 1),
    )
    return *results[: -2 * n], list(zip(results[-2 * n : -n], results[-n:]))


def centre(acts, outer, bias_conv):
    size, c = acts[0].shape
    m = outer.shape[2]
    n = len(acts)

    def body(*refs):
        outer_ref, bias_ref = refs[n : n + 2]
        for act_ref, out_ref in zip(refs[:n], refs[n + 2 :]):
            out_ref[...] = dot(act_ref[...], outer_ref[1]) + bias_ref[...]

    args = list(acts) + [outer, bias_conv]
    return call(body, "centre", [shape(size, m, F32)] * n, args, 2 * n * size * c * m, [], specs=[VMEM] * len(args))


def finish(quarter, at, centre_sum, one_side, other_side, one, point, bias_point, whole):
    size, c = one.shape
    rows, m = one_side.shape
    steps = 2 if rows % 256 == 0 else 1
    step = rows // steps

    def body(centre_ref, one_side_ref, other_side_ref, one_ref, point_ref, bias_ref, *rest):
        out_hbm, held, sems = rest[-3:]
        start = quarter_rows(quarter, size).start + at
        copies = []
        for k in range(steps):
            part, own = pl.ds(k * step, step), pl.ds(at + k * step, step)
            total = centre_ref[own, :] + one_side_ref[part, :].astype(F32) + other_side_ref[part, :].astype(F32)
            mid = gelu(total).astype(BF16)
            out = one_ref[own, :].astype(F32) + dot(mid, point_ref[...]) + bias_ref[...]
            held[k] = out.astype(BF16)
            to = pl.ds(pl.multiple_of(start + k * step, 32), step)
            copies.append(pltpu.make_async_copy(held.at[k], out_hbm.at[to], sems.at[k]))
            copies[k].start()
        for copy in copies:
            copy.wait()

    args = [centre_sum, one_side, other_side, one, point, bias_point] + ([] if whole is None else [whole])
    return call(
        body, f"finish{quarter}", [shape(4 * size, c)], args, 2 * rows * c * m,
        [pltpu.VMEM((steps, step, c), BF16), pltpu.SemaphoreType.DMA((steps,))],
        aliases={} if whole is None else {6: 0}, out_specs=[ANY], specs=[VMEM] * 6 + [ANY] * (len(args) - 6),
    )[0]


def per_device(
    tower_input,
    first_conv_taps,
    first_conv_bias,
    first_point_weight,
    first_point_bias,
    second_conv_taps,
    second_conv_bias,
    second_point_weight,
    second_point_bias,
):
    size = tower_input.shape[0] // 4
    whole = (size,)
    split = (size - LAST_PIECE, LAST_PIECE)

    near = (first_conv_taps, first_conv_bias[None, :], first_point_weight, first_point_bias[None, :], second_conv_taps)
    x = pltpu.with_memory_space_constraint(tower_input, pltpu.HBM)
    rim_taps = pltpu.with_memory_space_constraint(first_conv_taps, pltpu.HBM)

    def to_partner(value):
        return swap(value, lambda i: i % 2 == 0, 1)

    def second_matching(value):
        return swap(value, lambda i: i // 2 % 2 == 1, 2)

    def first_matching(value):
        return swap(value, lambda i: i // 2 % 2 == 0, 2)

    def send(products):
        return [(second_matching(second), first_matching(first)) for first, second in products]

    act0, to_pair = rim(x, rim_taps, 0, size)
    from_pair = swap(to_pair, lambda i: i % 2 == 1, 1)
    act1, act2, one1, far1, *products1 = first_quarter(tower_input, act0, near)
    later, products1 = lax.optimization_barrier((x, products1))
    sides1 = send([products1])
    act3, for_partner = rim(later, rim_taps, 3, size)
    from_partner = to_partner(for_partner)
    one2, far2, products2 = layer(x, 2, (act1, act2, act3), [], near, whole)
    sides2 = send(products2)
    one0, far0, products0 = layer(
        x, 0, (None, act0, act1), [(from_pair, 0)], near, whole
    )
    sides0 = send(products0)
    one3, far3, products3 = layer(x, 3, (act2, act3, None), [(from_partner, 0)], near, split)
    sides3 = send(products3)

    centres = centre((far1, far2, far0, far3), second_conv_taps, second_conv_bias[None, :])
    out = None
    for quarter, total, sides, one in zip(
        (1, 2, 0, 3), centres, (sides1, sides2, sides0, sides3), (one1, one2, one0, one3)
    ):
        at = 0
        for pair in sides:
            out = finish(quarter, at, total, *pair, one, second_point_weight, second_point_bias[None, :], out)
            at += pair[0].shape[0]
    return out


def solution(mesh):
    return jax.shard_map(
        per_device,
        mesh=mesh,
        in_specs=(P(("grp", "seq"), None), P(), P(), P(), P(), P(), P(), P(), P()),
        out_specs=P(("grp", "seq"), None),
        check_vma=False,
    )
```
